256 devices in a mesh: gx: 16 (over z, core), gy: 16 (over x, y).
Axes of the slice: x: 4, y: 4, z: 8, core: 2. Of those that a mesh axis runs over, the one named last changes fastest.
Arguments:
- features: bfloat16 [256, 256, 1, 1024], P('gx', 'gy'), may hold values from -6 to 6
- slot_map: int32 [16, 16, 2], replicated, may hold values from -1 to 0, as said below
- tap_weights: float32 [27, 64], replicated, may hold values from -1.25 to 1.25
- gain: float32 [64], replicated, may hold values from 0.5 to 1.5
- mix_weight: bfloat16 [64, 64], replicated, may hold values from -0.75 to 0.75
- cotangent: bfloat16 [256, 256, 1, 1024], P('gx', 'gy'), may hold values from -6 to 6
Outputs:
- mixed: bfloat16 [256, 256, 1, 1024], P('gx', 'gy')
- grad_features: bfloat16 [256, 256, 1, 1024], P('gx', 'gy')
- grad_taps: float32 [27, 64], replicated
- grad_gain: float32 [64], replicated
- grad_mix: float32 [64, 64], replicated
The draws below stay inside these ranges and needn't reach their ends.
Inputs may be any that keep to these rules, and one draw needn't show every extreme that they name: `slot_map`: in each block column the active levels carry slot numbers 0, 1, 2, ... in increasing level order and the others carry -1; every block column has exactly 1 active block.
All inputs are finite; a program needn't handle non-finite values.
Results may differ from the reference program's by a relative error of at most 0.0039.
Values may be sent and summed in bfloat16 or wider, within the bound.
A program may use at most 128 MiB of HBM per device.

```python
import jax
import jax.numpy as jnp
from jax import lax

BS = 16
CH = 64
BZ = 2
B_DEV = 1
NX = 256
NY = 256
LANES = 1024
N_GX = 16
N_GY = 16


def column_order(perm_key):
    return jax.random.permutation(perm_key, BZ)


def draw_slot_map(key, part):
    tile_total = N_GX * N_GY
    key_count, key_full, key_perm = jax.random.split(jax.random.fold_in(key, 7), 3)
    counts = jax.random.randint(key_count, (tile_total,), 1, B_DEV + 1)
    fullest = jax.random.randint(key_full, (), 0, tile_total)
    counts = jnp.where(jnp.arange(tile_total, dtype=jnp.int32) == fullest, B_DEV, counts)
    orders = jax.vmap(column_order)(jax.random.split(key_perm, tile_total)).astype(jnp.int32)
    ranks = jnp.argsort(orders, axis=1, stable=True).astype(jnp.int32)
    active = ranks < counts[:, None]
    slot_index = jnp.cumsum(active.astype(jnp.int32), axis=1) - 1
    result = jnp.where(active, slot_index, -1).astype(jnp.int32)
    return result.reshape(N_GX, N_GY, BZ)


def level_of(stream_key, dims, pieces, smallest, largest):
    factor_of = 1.0
    for dim, blocks in pieces:
        steps = jax.random.uniform(jax.random.fold_in(jax.random.fold_in(stream_key, 6), dim), (blocks,), jnp.float32, smallest / len(pieces), largest / len(pieces))
        factor_of = factor_of * jnp.repeat(jnp.exp(steps), dims[dim] // blocks).reshape((-1,) + (1,) * (len(dims) - 1 - dim))
    return factor_of


def centred(own_key, dims, width, bound, pieces=(), kind=jnp.bfloat16):
    values = width * jax.random.normal(own_key, dims, jnp.float32)
    if pieces:
        values = values * level_of(own_key, dims, pieces, -0.22, 0.18)
    return jnp.clip(values, -bound, bound).astype(kind)


def setup_inputs(seed: int = 0) -> dict:
    key_of = jax.random.split(jax.random.key(seed), 7)
    features = centred(key_of[0], (NX, NY, B_DEV, LANES), 1.0, 6.0, ((0, 16), (1, 16)))
    slot_map = draw_slot_map(jax.random.fold_in(key_of[6], 71), 0)
    tap_weights = centred(key_of[2], (27, CH), 27 ** -0.5, 1.25, (), jnp.float32)
    gain = jnp.clip(1.0 + 0.1 * jax.random.normal(key_of[3], (CH,), jnp.float32), 0.5, 1.5)
    mix_weight = centred(key_of[4], (CH, CH), CH ** -0.5, 0.75)
    cotangent = centred(key_of[5], (NX, NY, B_DEV, LANES), 1.0, 6.0, ((0, 16), (1, 16)))
    return {"features": features, "slot_map": slot_map, "tap_weights": tap_weights, "gain": gain, "mix_weight": mix_weight, "cotangent": cotangent}


EPS = 1e-05

def one_hot_map(level_slots, slot_count):
    slot_ids = jnp.arange(slot_count, dtype=jnp.int32)
    return (level_slots[..., None] == slot_ids).astype(jnp.float32)

def slot_lookup(center, slot_count):
    slot_ids = jnp.arange(slot_count, dtype=jnp.int32)
    matches = center[:, None] == slot_ids[None, :]
    level_ids = jnp.arange(center.shape[0], dtype=jnp.int32)[:, None]
    position = lax.optimization_barrier(jnp.sum(jnp.where(matches, level_ids, 0), axis=0)).astype(jnp.int32)
    active = jnp.any(matches, axis=0)
    return (position, active)

def spread_edges(table, inner, axis):
    first = lax.slice_in_dim(table, 0, 1, axis=axis)
    middle = jnp.repeat(lax.slice_in_dim(table, 1, 2, axis=axis), inner, axis=axis)
    last = lax.slice_in_dim(table, 2, 3, axis=axis)
    return jnp.concatenate([first, middle, last], axis=axis)

def extend_cells(block, near_maps):
    inner = block.shape[0] - 2
    table = one_hot_map(near_maps, block.shape[2])
    table = spread_edges(spread_edges(table, inner, 0), inner, 1)
    dense_cells = jnp.einsum('xysf,xyps->xypf', block.astype(jnp.float32), table, precision=lax.Precision.HIGHEST)
    return dense_cells.astype(jnp.bfloat16)

def widen(extended, channels):
    grid = extended.shape[0]
    flat = extended.reshape(grid, grid, -1)
    return jnp.pad(flat, ((0, 0), (0, 0), (channels, channels)))

def stencil(padded, taps):
    channels = taps.shape[1]
    inner = padded.shape[0] - 2
    length = padded.shape[2] - 2 * channels
    accum_sum = jnp.zeros((inner, inner, length), jnp.float32)
    for tap_index in range(27):
        off_x = tap_index // 9
        off_y = tap_index // 3 % 3
        off_z = tap_index % 3
        shifted = padded[off_x:off_x + inner, off_y:off_y + inner, channels * off_z:channels * off_z + length].astype(jnp.float32)
        accum_sum = accum_sum + shifted * jnp.tile(taps[tap_index], length // channels)
    return accum_sum

def tap_grads(padded, grads, channels):
    inner = padded.shape[0] - 2
    length = padded.shape[2] - 2 * channels
    rows_out = []
    for tap_index in range(27):
        off_x = tap_index // 9
        off_y = tap_index // 3 % 3
        off_z = tap_index % 3
        shifted = padded[off_x:off_x + inner, off_y:off_y + inner, channels * off_z:channels * off_z + length].astype(jnp.float32)
        rows_out.append(lax.optimization_barrier(jnp.sum((shifted * grads).reshape(-1, channels), axis=0)))
    return jnp.stack(rows_out)

def norm_forward(depth_slots):
    mean_square = lax.optimization_barrier(jnp.mean(depth_slots * depth_slots, axis=-1, keepdims=True))
    inv_rms = lax.rsqrt(mean_square + EPS)
    return (depth_slots * inv_rms, inv_rms)

def norm_backward(grad_norm, normed, inv_rms, gain):
    grad_scaled = grad_norm * gain
    return inv_rms * (grad_scaled - normed * lax.optimization_barrier(jnp.mean(grad_scaled * normed, axis=-1, keepdims=True)))

def reference(features, slot_map, tap_weights, gain, mix_weight, cotangent):
    lane_width = BS * CH
    cell_shape = (BS, BS, B_DEV, BS, CH)
    padded_feat = jnp.pad(features, ((1, 1), (1, 1), (0, 0), (0, 0)))
    padded_map = jnp.pad(slot_map, ((1, 1), (1, 1), (0, 0)), constant_values=-1)
    tile_ids = jnp.arange(N_GX * N_GY, dtype=jnp.int32)

    def locate(tile):
        grid_row = tile // N_GY
        grid_col = tile % N_GY
        near_maps = lax.dynamic_slice(padded_map, (grid_row, grid_col, jnp.int32(0)), (3, 3, BZ))
        start = (grid_row * BS, grid_col * BS, jnp.int32(0), jnp.int32(0))
        return (near_maps, start)

    def forward_tile(tile):
        near_maps, start = locate(tile)
        slab = lax.dynamic_slice(padded_feat, start, (BS + 2, BS + 2, B_DEV, lane_width))
        own_grad = lax.dynamic_slice(cotangent, start, (BS, BS, B_DEV, lane_width))
        position, active = slot_lookup(near_maps[1, 1], B_DEV)
        keep_mask = active.astype(jnp.float32)[None, None, :, None, None]
        padded_in = widen(extend_cells(slab, near_maps), CH)
        depth_field = stencil(padded_in, tap_weights).reshape(BS, BS, BZ, lane_width)
        depth_slots = jnp.take(depth_field, position, axis=2).reshape(cell_shape)
        normed, inv_rms = norm_forward(depth_slots)
        norm_bf = (normed * gain).astype(jnp.bfloat16)
        branch = jnp.einsum('xyszc,cd->xyszd', norm_bf.astype(jnp.float32), mix_weight.astype(jnp.float32), precision=lax.Precision.HIGHEST)
        inputs_f = slab[1:-1, 1:-1].reshape(cell_shape).astype(jnp.float32)
        mixed = ((inputs_f + branch) * keep_mask).astype(jnp.bfloat16).reshape(BS, BS, B_DEV, lane_width)
        grad_out = own_grad.reshape(cell_shape) * keep_mask.astype(jnp.bfloat16)
        grad_mix_part = jnp.einsum('xyszc,xyszd->cd', norm_bf.astype(jnp.float32), grad_out.astype(jnp.float32), precision=lax.Precision.HIGHEST)
        grad_norm = jnp.einsum('xyszd,cd->xyszc', grad_out.astype(jnp.float32), mix_weight.astype(jnp.float32), precision=lax.Precision.HIGHEST)
        grad_gain_part = lax.optimization_barrier(jnp.sum(grad_norm * normed, axis=(0, 1, 2, 3)))
        grad_depth = (norm_backward(grad_norm, normed, inv_rms, gain) * keep_mask).astype(jnp.bfloat16)
        return (mixed, grad_depth.reshape(BS, BS, B_DEV, lane_width), grad_mix_part, grad_gain_part)

    def assemble(tiles):
        shaped = tiles.reshape(N_GX, N_GY, BS, BS, B_DEV, lane_width).transpose(0, 2, 1, 3, 4, 5)
        return shaped.reshape(N_GX * BS, N_GY * BS, B_DEV, lane_width)
    mixed_tiles, depth_tiles, mix_parts, gain_parts = lax.map(forward_tile, tile_ids)
    padded_depth = jnp.pad(assemble(depth_tiles), ((1, 1), (1, 1), (0, 0), (0, 0)))

    def backward_tile(tile):
        near_maps, start = locate(tile)
        slab = lax.dynamic_slice(padded_feat, start, (BS + 2, BS + 2, B_DEV, lane_width))
        slab_grad = lax.dynamic_slice(padded_depth, start, (BS + 2, BS + 2, B_DEV, lane_width))
        own_grad = lax.dynamic_slice(cotangent, start, (BS, BS, B_DEV, lane_width))
        position, active = slot_lookup(near_maps[1, 1], B_DEV)
        keep_mask = active.astype(jnp.float32)[None, None, :, None, None]
        padded_in = widen(extend_cells(slab, near_maps), CH)
        padded_grad = widen(extend_cells(slab_grad, near_maps), CH)
        back_field = stencil(padded_grad, tap_weights[::-1]).reshape(BS, BS, BZ, lane_width)
        back_slots = jnp.take(back_field, position, axis=2)
        grad_feat = ((own_grad.astype(jnp.float32) + back_slots).reshape(cell_shape) * keep_mask).astype(jnp.bfloat16)
        grad_center = padded_grad[1:-1, 1:-1, CH:-CH].astype(jnp.float32)
        taps_part = tap_grads(padded_in, grad_center, CH)
        return (grad_feat.reshape(BS, BS, B_DEV, lane_width), taps_part)
    grad_tiles, taps_parts = lax.map(backward_tile, tile_ids)
    return (assemble(mixed_tiles), assemble(grad_tiles), lax.optimization_barrier(jnp.sum(taps_parts, axis=0)), lax.optimization_barrier(jnp.sum(gain_parts, axis=0)), lax.optimization_barrier(jnp.sum(mix_parts, axis=0)))
```

```python
import functools

import jax
import jax.numpy as jnp
from jax import lax
from jax.experimental import pallas as pl
from jax.experimental.pallas import tpu as pltpu
from jax.sharding import PartitionSpec as P

EPS = 1e-05
MESH = pl.DeviceIdType.MESH
F32 = jnp.float32
BF16 = jnp.bfloat16
SIDE = 16
CH = 64
KT = 8
LANES = KT * 128
ROWS = 32
SLOT = KT * ROWS
FIELD = (SIDE + 2) * SLOT
Y0 = 8
OFFSETS = (-1, 0, 1)


def zrow(oz, slot, tile):
    return oz * FIELD + slot * SLOT + tile * ROWS


def shifted_tiles(tiles, low):
    count = len(tiles)
    rot = [pltpu.roll(tile, CH, 1) for tile in tiles]
    down = [jnp.where(low, rot[k - 1], rot[k]) for k in range(count)]
    up = [jnp.where(low, rot[k], rot[(k + 1) % count]) for k in range(count)]
    return down, up


def fill_own(src, field, low):
    @pl.loop(0, SIDE)
    def _(x):
        tiles = [src[x, :, k * 128 : (k + 1) * 128].astype(F32) for k in range(KT)]
        down, up = shifted_tiles(tiles, low)
        down[0] = jnp.where(low, 0.0, down[0])
        up[-1] = jnp.where(low, up[-1], 0.0)
        for oz, values in enumerate((down, tiles, up)):
            rows = field.at[pl.ds(pl.multiple_of(oz * FIELD + (x + 1) * SLOT, SLOT), SLOT)]
            for k in range(KT):
                rows[k * ROWS + Y0 : k * ROWS + Y0 + SIDE, :] = values[k]


def gather_edges(field, ysend, csend):
    for side in range(2):
        row = Y0 + side * (SIDE - 1)
        for k in range(KT):
            column = field[pl.ds(zrow(1, 1, k) + row, SIDE, stride=SLOT), :]
            ysend[side, :, k * 128 : (k + 1) * 128] = column.astype(BF16)
    for hx in range(2):
        for hy in range(2):
            start = zrow(1, 1 + hx * (SIDE - 1), 0) + Y0 + hy * (SIDE - 1)
            csend[2 * hx + hy] = field[pl.ds(start, KT, stride=ROWS), :]


def fill_halo(field, xrecv, yrecv, crecv, masks, low):
    def masked(tiles, mask):
        same, below, above = mask
        down, up = shifted_tiles(tiles, low)
        first = jnp.where(low, below, same)
        last = jnp.where(low, same, above)
        down = [v * (first if k == 0 else same) for k, v in enumerate(down)]
        up = [v * (last if k == KT - 1 else same) for k, v in enumerate(up)]
        return down, [v * same for v in tiles], up

    for side in range(2):
        tiles = [xrecv[side, :, k * 128 : (k + 1) * 128].astype(F32) for k in range(KT)]
        for oz, values in enumerate(masked(tiles, masks[(2 * side - 1, 0)])):
            for k in range(KT):
                start = zrow(oz, side * (SIDE + 1), k) + Y0
                field[start : start + SIDE, :] = values[k]
        tiles = [yrecv[side, :, k * 128 : (k + 1) * 128].astype(F32) for k in range(KT)]
        for oz, values in enumerate(masked(tiles, masks[(0, 2 * side - 1)])):
            for k in range(KT):
                start = zrow(oz, 1, k) + (Y0 - 1, Y0 + SIDE)[side]
                field[pl.ds(start, SIDE, stride=SLOT), :] = values[k]
    low8 = low[:KT]
    row8 = lax.broadcasted_iota(jnp.int32, (KT, 128), 0)
    for hx in range(2):
        for hy in range(2):
            same, below, above = masks[(2 * hx - 1, 2 * hy - 1)]
            cell = crecv[2 * hx + hy]
            rot = pltpu.roll(cell, CH, 1)
            down = jnp.where(low8, pltpu.roll(rot, 1, 0), rot)
            up = jnp.where(low8, rot, pltpu.roll(rot, KT - 1, 0))
            down = down * jnp.where(low8 & (row8 == 0), below, same)
            up = up * jnp.where((~low8) & (row8 == KT - 1), above, same)
            for oz, value in enumerate((down, cell * same, up)):
                start = zrow(oz, hx * (SIDE + 1), 0) + (Y0 - 1, Y0 + SIDE)[hy]
                field[pl.ds(start, KT, stride=ROWS), :] = value


def stencil(field, weights, result, finish=None):
    @pl.loop(0, KT)
    def _(k):
        rows = field.at[pl.ds(pl.multiple_of(k * ROWS, ROWS), 3 * FIELD - (KT - 1) * ROWS)]
        for half in range(2):
            sums = {}
            for slot in range(SIDE + 2):
                for oz in OFFSETS:
                    for oy in OFFSETS:
                        start = (oz + 1) * FIELD + slot * SLOT + Y0 + 8 * half + oy
                        value = rows[start : start + 8, :]
                        for ox in OFFSETS:
                            x = slot - 1 - ox
                            if 0 <= x < SIDE:
                                term = value * weights[9 * (ox + 1) + 3 * (oy + 1) + oz + 1]
                                sums[x] = sums[x] + term if x in sums else term
                if slot >= 2:
                    result[slot - 2, k, 8 * half : 8 * half + 8, :] = sums.pop(slot - 2)
        if finish is not None:
            finish(k)


def tap_products(field, grads):
    def body(k, totals):
        totals = list(totals)
        span = FIELD - (KT - 1) * ROWS
        base = pl.multiple_of(k * ROWS, ROWS)
        rows = field.at[pl.ds(base, 2 * FIELD + span)]
        centre = grads.at[pl.ds(base + FIELD, span)]
        for half in range(2):
            for slot in range(SIDE + 2):
                near = {}
                for ox in OFFSETS:
                    x = slot - 1 - ox
                    if 0 <= x < SIDE:
                        start = (x + 1) * SLOT + Y0 + 8 * half
                        near[ox] = centre[start : start + 8, :]
                for oz in OFFSETS:
                    for oy in OFFSETS:
                        start = (oz + 1) * FIELD + slot * SLOT + Y0 + 8 * half + oy
                        value = rows[start : start + 8, :]
                        for ox, grad in near.items():
                            tap = 9 * (ox + 1) + 3 * (oy + 1) + oz + 1
                            totals[tap] = totals[tap] + value * grad
        return tuple(totals)

    zero = jnp.zeros((8, 128), F32)
    return lax.fori_loop(0, KT, body, (zero,) * 27)


def kernel(
    n_gx, n_gy,
    feat_hbm, map_ref, taps_ref, gain_ref, mix_ref, cot_hbm,
    mixed_hbm, gf_hbm, gt_ref, gg_ref, gm_ref,
    feat, cot, mixed, gf, gd, field, gfield, depth, tapsb, wdiag, mixacc, gainacc,
    xrecv1, yrecv1, crecv1, xrecv2, yrecv2, crecv2, ysend, csend, ysend2, csend2,
    pbuf, red, recv1, part2, recv2, part3, gath,
    io_sem, send1, land1, send2, land2, rsend, rland,
):
    gx = lax.axis_index("gx")
    gy = lax.axis_index("gy")

    load_feat = pltpu.make_async_copy(feat_hbm, feat, io_sem.at[0])
    load_cot = pltpu.make_async_copy(cot_hbm, cot, io_sem.at[1])
    load_feat.start()
    load_cot.start()

    def peer_x(d):
        return lax.rem(gx + d + n_gx, n_gx)

    def peer_y(d):
        return lax.rem(gy + d + n_gy, n_gy)

    barrier = pltpu.get_barrier_semaphore()

    @pl.loop(1, n_gx)
    def _(d):
        pl.semaphore_signal(barrier, inc=1, device_id=(peer_x(d), gy), device_id_type=MESH)

    @pl.loop(1, n_gy)
    def _(d):
        pl.semaphore_signal(barrier, inc=1, device_id=(gx, peer_y(d)), device_id_type=MESH)

    for dx in (-1, 1):
        for dy in (-1, 1):
            pl.semaphore_signal(
                barrier, inc=1, device_id=(peer_x(dx), peer_y(dy)), device_id_type=MESH
            )

    low = lax.broadcasted_iota(jnp.int32, (SIDE, 128), 1) < CH
    low8 = low[:8]

    def level(i, j):
        return jnp.where(map_ref[i, j, 1] == 0, 1, 0)

    own_level = level(gx, gy)
    masks = {}
    for dx in OFFSETS:
        for dy in OFFSETS:
            if dx == 0 and dy == 0:
                continue
            inside = (gx + dx >= 0) & (gx + dx < n_gx) & (gy + dy >= 0) & (gy + dy < n_gy)
            delta = level(peer_x(dx), peer_y(dy)) - own_level
            masks[(dx, dy)] = tuple(
                jnp.where(inside & (delta == step), 1.0, 0.0).astype(F32) for step in (0, -1, 1)
            )

    taps2 = jnp.concatenate([taps_ref[...], taps_ref[...]], axis=1)
    for tap in range(27):
        tapsb[8 * tap : 8 * tap + 8, :] = jnp.broadcast_to(taps2[tap : tap + 1, :], (8, 128))
    gain2 = jnp.concatenate([gain_ref[...], gain_ref[...]], axis=1)
    gain4 = jnp.concatenate([gain2, gain2], axis=1)
    row_block = lax.broadcasted_iota(jnp.int32, (4 * CH, 4 * CH), 0) // CH
    col_block = lax.broadcasted_iota(jnp.int32, (4 * CH, 4 * CH), 1) // CH
    diagonal = row_block == col_block
    wide = jnp.concatenate([mix_ref[...].astype(F32)] * 2, axis=1)
    wide = jnp.concatenate([wide, wide], axis=1)
    wide = jnp.concatenate([wide] * 4, axis=0)
    wdiag[0] = jnp.where(diagonal, wide, 0.0).astype(BF16)
    wdiag[1] = jnp.where(diagonal, 1.0 / CH, 0.0).astype(BF16)
    mixacc[...] = jnp.zeros_like(mixacc)
    gainacc[...] = jnp.zeros_like(gainacc)

    load_feat.wait()
    fill_own(feat, field, low)
    gather_edges(field, ysend, csend)

    def halo_copies(src, ys, cs, xr, yr, cr, send, land):
        copies = []
        for step in (-1, 1):
            far = (step + 1) // 2
            copies.append((src.at[far * (SIDE - 1)], xr.at[1 - far], (peer_x(step), gy)))
            copies.append((ys.at[far], yr.at[1 - far], (gx, peer_y(step))))
        for dx in (-1, 1):
            for dy in (-1, 1):
                here = (dx + 1) + (dy + 1) // 2
                copies.append((cs.at[here], cr.at[3 - here], (peer_x(dx), peer_y(dy))))
        return [
            pltpu.make_async_remote_copy(
                src_ref=a, dst_ref=b, send_sem=send.at[n], recv_sem=land.at[n],
                device_id=to, device_id_type=MESH,
            )
            for n, (a, b, to) in enumerate(copies)
        ]

    pl.semaphore_wait(barrier, (n_gx - 1) + (n_gy - 1) + 4)
    halo1 = halo_copies(feat, ysend, csend, xrecv1, yrecv1, crecv1, send1, land1)
    for copy in halo1:
        copy.start()
    for copy in halo1:
        copy.wait()
    fill_halo(field, xrecv1, yrecv1, crecv1, masks, low)

    weights = [tapsb[8 * tap : 8 * tap + 8, :] for tap in range(27)]
    stencil(field, weights, depth)

    load_cot.wait()
    cells = SIDE * SIDE

    @pl.loop(0, KT // 2)
    def _(m):
        lanes = pl.ds(pl.multiple_of(m * 256, 256), 256)
        values = jnp.concatenate(
            [depth[:, 2 * m + h].reshape(cells, 128) for h in range(2)], axis=1
        )
        mean_square = jnp.dot((values * values).astype(BF16), wdiag[1], preferred_element_type=F32)
        inv_rms = lax.rsqrt(mean_square + EPS)
        normed = values * inv_rms
        norm_bf = (normed * gain4).astype(BF16)
        branch = jnp.dot(norm_bf, wdiag[0], preferred_element_type=F32)
        inputs = feat[:, :, lanes].reshape(cells, 256).astype(F32)
        mixed[:, :, lanes] = (inputs + branch).astype(BF16).reshape(SIDE, SIDE, 256)
        grad_out = cot[:, :, lanes].reshape(cells, 256)
        grad_norm = lax.dot_general(
            grad_out, wdiag[0], (((1,), (1,)), ((), ())), preferred_element_type=F32
        )
        product = grad_norm * normed
        gainacc[...] += jnp.sum(product.reshape(cells // 8, 8, 256), axis=0)
        mean = jnp.dot((product * gain4).astype(BF16), wdiag[1], preferred_element_type=F32)
        grad_depth = inv_rms * (grad_norm * gain4 - normed * mean)
        gd[:, :, lanes] = grad_depth.astype(BF16).reshape(SIDE, SIDE, 256)
        mixacc[...] += lax.dot_general(
            norm_bf, grad_out, (((0,), (0,)), ((), ())), preferred_element_type=F32
        )

    store_mixed = pltpu.make_async_copy(mixed, mixed_hbm, io_sem.at[2])
    store_mixed.start()

    fill_own(gd, gfield, low)
    gather_edges(gfield, ysend2, csend2)
    halo2 = halo_copies(gd, ysend2, csend2, xrecv2, yrecv2, crecv2, send2, land2)
    for copy in halo2:
        copy.start()

    totals = list(tap_products(field, gfield))
    totals.append(gainacc[:, :128] + gainacc[:, 128:])
    folded = [total + pltpu.roll(total, CH, 1) for total in totals]
    for j in range(14):
        pair = jnp.where(low8, folded[2 * j], folded[2 * j + 1])
        pbuf[j : j + 1, :] = jnp.sum(pair, axis=0, keepdims=True)
    pbuf[14:16, :] = jnp.zeros((2, 128), F32)
    even = mixacc[0:CH, 0:128] + mixacc[2 * CH : 3 * CH, 128:256]
    odd = mixacc[CH : 2 * CH, 0:128] + mixacc[3 * CH : 4 * CH, 128:256]
    wide_low = lax.broadcasted_iota(jnp.int32, (CH, 128), 1) < CH
    both = jnp.where(wide_low, even, odd)
    both = both + pltpu.roll(both, CH, 1)
    pbuf[16:48, :] = jnp.where(wide_low[:32], both[:32], both[32:])

    per_peer = 48 // n_gx
    red[...] = jnp.zeros_like(red)
    for q in range(per_peer):
        red[:, q, :] = pbuf[n_gx * q : n_gx * q + n_gx, :]

    def remote(src, dst, index, to):
        return pltpu.make_async_remote_copy(
            src_ref=src, dst_ref=dst, send_sem=rsend.at[index], recv_sem=rland.at[index],
            device_id=to, device_id_type=MESH,
        )

    def landed(buffer, index):
        pltpu.make_async_copy(buffer, buffer, rland.at[index]).wait()

    @pl.loop(1, n_gx)
    def _(d):
        remote(red.at[peer_x(d)], recv1.at[d - 1], 0, (peer_x(d), gy)).start()

    landed(recv1, 0)
    part2[...] = red[gx] + jnp.sum(recv1[...], axis=0)
    recv2[gy] = part2[...]

    @pl.loop(1, n_gy)
    def _(d):
        remote(part2, recv2.at[gy], 1, (gx, peer_y(d))).start()

    for copy in halo2:
        copy.wait()
    fill_halo(gfield, xrecv2, yrecv2, crecv2, masks, low)

    def finish(k):
        lanes = pl.ds(pl.multiple_of(k * 128, 128), 128)
        for x in range(SIDE):
            total = cot[x, :, lanes].astype(F32) + depth[x, k]
            gf[x, :, lanes] = total.astype(BF16)

    stencil(gfield, weights[::-1], depth, finish)
    store_gf = pltpu.make_async_copy(gf, gf_hbm, io_sem.at[3])
    store_gf.start()

    landed(recv2.at[pl.ds(0, n_gy - 1)], 1)
    part3[...] = jnp.sum(recv2[...], axis=0)
    gath[gx] = part3[...]

    @pl.loop(1, n_gx)
    def _(d):
        remote(part3, gath.at[gx], 2, (peer_x(d), gy)).start()

    landed(gath.at[pl.ds(0, n_gx - 1)], 2)
    for q in range(per_peer):
        pbuf[n_gx * q : n_gx * q + n_gx, :] = gath[:, q, :]
    rows = pbuf[0:16, :]
    turned = pltpu.roll(rows, CH, 1)
    for tap in range(27):
        source = turned if tap % 2 else rows
        gt_ref[tap : tap + 1, :] = source[tap // 2 : tap // 2 + 1, :CH]
    gg_ref[...] = turned[13:14, :CH]
    packed = pbuf[16:48, :]
    gm_ref[0:32, :] = packed[:, :CH]
    gm_ref[32:64, :] = pltpu.roll(packed, CH, 1)[:, :CH]

    def sent(buffer, index):
        pltpu.make_async_copy(buffer, buffer, rsend.at[index]).wait()

    sent(recv1, 0)
    sent(recv2.at[pl.ds(0, n_gy - 1)], 1)
    sent(gath.at[pl.ds(0, n_gx - 1)], 2)
    store_mixed.wait()
    store_gf.wait()


def shards(n_gx, n_gy, features, slot_map, tap_weights, gain, mix_weight, cotangent):
    block = (SIDE, SIDE, LANES)
    padded = max(4, 48 // n_gx)
    vmem = pl.BlockSpec(memory_space=pltpu.VMEM)
    hbm = pl.BlockSpec(memory_space=pl.ANY)
    smem = pl.BlockSpec(memory_space=pltpu.SMEM)
    halo = [
        pltpu.VMEM((2, SIDE, LANES), BF16),
        pltpu.VMEM((2, SIDE, LANES), BF16),
        pltpu.VMEM((4, KT, 128), F32),
    ]
    mixed, grad_features, grad_taps, grad_gain, grad_mix = pl.pallas_call(
        functools.partial(kernel, n_gx, n_gy),
        out_shape=(
            jax.ShapeDtypeStruct(block, BF16),
            jax.ShapeDtypeStruct(block, BF16),
            jax.ShapeDtypeStruct((27, CH), F32),
            jax.ShapeDtypeStruct((1, CH), F32),
            jax.ShapeDtypeStruct((CH, CH), F32),
        ),
        in_specs=[hbm, smem, vmem, vmem, vmem, hbm],
        out_specs=(hbm, hbm, vmem, vmem, vmem),
        scratch_shapes=[pltpu.VMEM(block, BF16)] * 5
        + [pltpu.VMEM((3 * FIELD, 128), F32)] * 2
        + [
            pltpu.VMEM((SIDE, KT, SIDE, 128), F32),
            pltpu.VMEM((27 * 8, 128), F32),
            pltpu.VMEM((2, 4 * CH, 4 * CH), BF16),
            pltpu.VMEM((4 * CH, 4 * CH), F32),
            pltpu.VMEM((8, 4 * CH), F32),
        ]
        + halo
        + halo
        + halo[1:]
        + halo[1:]
        + [
            pltpu.VMEM((48, 128), F32),
            pltpu.VMEM((n_gx, padded, 128), F32),
            pltpu.VMEM((n_gx - 1, padded, 128), F32),
            pltpu.VMEM((padded, 128), F32),
            pltpu.VMEM((n_gy, padded, 128), F32),
            pltpu.VMEM((padded, 128), F32),
            pltpu.VMEM((n_gx, padded, 128), F32),
            pltpu.SemaphoreType.DMA((4,)),
            pltpu.SemaphoreType.DMA((8,)),
            pltpu.SemaphoreType.DMA((8,)),
            pltpu.SemaphoreType.DMA((8,)),
            pltpu.SemaphoreType.DMA((8,)),
            pltpu.SemaphoreType.DMA((3,)),
            pltpu.SemaphoreType.DMA((3,)),
        ],
        compiler_params=pltpu.CompilerParams(
            collective_id=0, has_side_effects=True, vmem_limit_bytes=48 * 1024 * 1024
        ),
        name="block_conv",
    )(
        features.reshape(block), slot_map, tap_weights, gain.reshape(1, CH), mix_weight,
        cotangent.reshape(block),
    )
    return (
        mixed.reshape(features.shape), grad_features.reshape(features.shape),
        grad_taps, grad_gain.reshape(CH), grad_mix,
    )


def solution(mesh):
    return jax.shard_map(
        functools.partial(shards, mesh.shape["gx"], mesh.shape["gy"]),
        mesh=mesh,
        in_specs=(P("gx", "gy", None, None), P(), P(), P(), P(), P("gx", "gy", None, None)),
        out_specs=(P("gx", "gy", None, None), P("gx", "gy", None, None), P(), P(), P()),
        check_vma=False,
    )
```

```python
import functools

import jax
import jax.numpy as jnp
from jax import lax
from jax.experimental import pallas as pl
from jax.experimental.pallas import tpu as pltpu
from jax.sharding import PartitionSpec as P

EPS = 1e-05
MESH = pl.DeviceIdType.MESH
F32 = jnp.float32
BF16 = jnp.bfloat16
SIDE = 16
CH = 64
KT = 8
LANES = KT * 128
ROWS = 32
SLOT = KT * ROWS
FIELD = (SIDE + 2) * SLOT
Y0 = 8
OFFSETS = (-1, 0, 1)


def zrow(oz, slot, tile):
    return oz * FIELD + slot * SLOT + tile * ROWS


def shifted_tiles(tiles, low):
    count = len(tiles)
    rot = [pltpu.roll(tile, CH, 1) for tile in tiles]
    down = [jnp.where(low, rot[k - 1], rot[k]) for k in range(count)]
    up = [jnp.where(low, rot[k], rot[(k + 1) % count]) for k in range(count)]
    return down, up


def fill_own(src, field, low):
    @pl.loop(0, SIDE)
    def _(x):
        tiles = [src[x, :, k * 128 : (k + 1) * 128].astype(F32) for k in range(KT)]
        down, up = shifted_tiles(tiles, low)
        down[0] = jnp.where(low, 0.0, down[0])
        up[-1] = jnp.where(low, up[-1], 0.0)
        for oz, values in enumerate((down, tiles, up)):
            rows = field.at[pl.ds(pl.multiple_of(oz * FIELD + (x + 1) * SLOT, SLOT), SLOT)]
            for k in range(KT):
                rows[k * ROWS + Y0 : k * ROWS + Y0 + SIDE, :] = values[k]


def gather_edges(field, ysend, csend):
    for side in range(2):
        row = Y0 + side * (SIDE - 1)
        for k in range(KT):
            column = field[pl.ds(zrow(1, 1, k) + row, SIDE, stride=SLOT), :]
            ysend[side, :, k * 128 : (k + 1) * 128] = column.astype(BF16)
    for hx in range(2):
        for hy in range(2):
            start = zrow(1, 1 + hx * (SIDE - 1), 0) + Y0 + hy * (SIDE - 1)
            csend[2 * hx + hy] = field[pl.ds(start, KT, stride=ROWS), :]


def fill_halo(field, xrecv, yrecv, crecv, masks, low):
    def masked(tiles, mask):
        same, below, above = mask
        down, up = shifted_tiles(tiles, low)
        first = jnp.where(low, below, same)
        last = jnp.where(low, same, above)
        down = [v * (first if k == 0 else same) for k, v in enumerate(down)]
        up = [v * (last if k == KT - 1 else same) for k, v in enumerate(up)]
        return down, [v * same for v in tiles], up

    for side in range(2):
        tiles = [xrecv[side, :, k * 128 : (k + 1) * 128].astype(F32) for k in range(KT)]
        for oz, values in enumerate(masked(tiles, masks[(2 * side - 1, 0)])):
            for k in range(KT):
                start = zrow(oz, side * (SIDE + 1), k) + Y0
                field[start : start + SIDE, :] = values[k]
        tiles = [yrecv[side, :, k * 128 : (k + 1) * 128].astype(F32) for k in range(KT)]
        for oz, values in enumerate(masked(tiles, masks[(0, 2 * side - 1)])):
            for k in range(KT):
                start = zrow(oz, 1, k) + (Y0 - 1, Y0 + SIDE)[side]
                field[pl.ds(start, SIDE, stride=SLOT), :] = values[k]
    low8 = low[:KT]
    row8 = lax.broadcasted_iota(jnp.int32, (KT, 128), 0)
    for hx in range(2):
        for hy in range(2):
            same, below, above = masks[(2 * hx - 1, 2 * hy - 1)]
            cell = crecv[2 * hx + hy]
            rot = pltpu.roll(cell, CH, 1)
            down = jnp.where(low8, pltpu.roll(rot, 1, 0), rot)
            up = jnp.where(low8, rot, pltpu.roll(rot, KT - 1, 0))
            down = down * jnp.where(low8 & (row8 == 0), below, same)
            up = up * jnp.where((~low8) & (row8 == KT - 1), above, same)
            for oz, value in enumerate((down, cell * same, up)):
                start = zrow(oz, hx * (SIDE + 1), 0) + (Y0 - 1, Y0 + SIDE)[hy]
                field[pl.ds(start, KT, stride=ROWS), :] = value


def stencil(field, weights, result, finish=None):
    @pl.loop(0, KT)
    def _(k):
        rows = field.at[pl.ds(pl.multiple_of(k * ROWS, ROWS), 3 * FIELD - (KT - 1) * ROWS)]
        for half in range(2):
            sums = {}
            for slot in range(SIDE + 2):
                for oz in OFFSETS:
                    for oy in OFFSETS:
                        start = (oz + 1) * FIELD + slot * SLOT + Y0 + 8 * half + oy
                        value = rows[start : start + 8, :]
                        for ox in OFFSETS:
                            x = slot - 1 - ox
                            if 0 <= x < SIDE:
                                term = value * weights[9 * (ox + 1) + 3 * (oy + 1) + oz + 1]
                                sums[x] = sums[x] + term if x in sums else term
                if slot >= 2:
                    result[slot - 2, k, 8 * half : 8 * half + 8, :] = sums.pop(slot - 2)
        if finish is not None:
            finish(k)


def tap_products(field, grads):
    def body(k, totals):
        totals = list(totals)
        span = FIELD - (KT - 1) * ROWS
        base = pl.multiple_of(k * ROWS, ROWS)
        rows = field.at[pl.ds(base, 2 * FIELD + span)]
        centre = grads.at[pl.ds(base + FIELD, span)]
        for half in range(2):
            for slot in range(SIDE + 2):
                near = {}
                for ox in OFFSETS:
                    x = slot - 1 - ox
                    if 0 <= x < SIDE:
                        start = (x + 1) * SLOT + Y0 + 8 * half
                        near[ox] = centre[start : start + 8, :]
                for oz in OFFSETS:
                    for oy in OFFSETS:
                        start = (oz + 1) * FIELD + slot * SLOT + Y0 + 8 * half + oy
                        value = rows[start : start + 8, :]
                        for ox, grad in near.items():
                            tap = 9 * (ox + 1) + 3 * (oy + 1) + oz + 1
                            totals[tap] = totals[tap] + value * grad
        return tuple(totals)

    zero = jnp.zeros((8, 128), F32)
    return lax.fori_loop(0, KT, body, (zero,) * 27)


def kernel(
    n_gx, n_gy,
    feat_hbm, map_ref, taps_hbm, gain_hbm, mix_hbm, cot_hbm,
    mixed, gf, pbuf,
    taps_ref, gain_ref, mix_ref, feat, cot, gd, field, gfield, depth, tapsb, wdiag, mixacc, gainacc,
    xrecv1, yrecv1, crecv1, xrecv2, yrecv2, crecv2, ysend, csend, ysend2, csend2,
    red, recv1, part2, recv2, part3, gath,
    io_sem, send1, land1, send2, land2, rsend, rland,
):
    gx = lax.axis_index("gx")
    gy = lax.axis_index("gy")

    load_feat = pltpu.make_async_copy(feat_hbm, feat, io_sem.at[0])
    load_cot = pltpu.make_async_copy(cot_hbm, cot, io_sem.at[1])
    load_params = [
        pltpu.make_async_copy(src, dst, io_sem.at[2 + n])
        for n, (src, dst) in enumerate(
            ((taps_hbm, taps_ref), (gain_hbm, gain_ref), (mix_hbm, mix_ref))
        )
    ]
    load_feat.start()
    for copy in load_params:
        copy.start()
    load_cot.start()

    def peer_x(d):
        return lax.rem(gx + d + n_gx, n_gx)

    def peer_y(d):
        return lax.rem(gy + d + n_gy, n_gy)

    barrier = pltpu.get_barrier_semaphore()

    @pl.loop(1, n_gx)
    def _(d):
        pl.semaphore_signal(barrier, inc=1, device_id=(peer_x(d), gy), device_id_type=MESH)

    @pl.loop(1, n_gy)
    def _(d):
        pl.semaphore_signal(barrier, inc=1, device_id=(gx, peer_y(d)), device_id_type=MESH)

    for dx in (-1, 1):
        for dy in (-1, 1):
            pl.semaphore_signal(
                barrier, inc=1, device_id=(peer_x(dx), peer_y(dy)), device_id_type=MESH
            )

    low = lax.broadcasted_iota(jnp.int32, (SIDE, 128), 1) < CH
    low8 = low[:8]

    def level(i, j):
        return jnp.where(map_ref[i, 1, j] == 0, 1, 0)

    own_level = level(gx, gy)
    masks = {}
    for dx in OFFSETS:
        for dy in OFFSETS:
            if dx == 0 and dy == 0:
                continue
            inside = (gx + dx >= 0) & (gx + dx < n_gx) & (gy + dy >= 0) & (gy + dy < n_gy)
            delta = level(peer_x(dx), peer_y(dy)) - own_level
            masks[(dx, dy)] = tuple(
                jnp.where(inside & (delta == step), 1.0, 0.0).astype(F32) for step in (0, -1, 1)
            )

    for copy in load_params:
        copy.wait()
    taps2 = jnp.concatenate([taps_ref[...], taps_ref[...]], axis=1)
    for tap in range(27):
        tapsb[8 * tap : 8 * tap + 8, :] = jnp.broadcast_to(taps2[tap : tap + 1, :], (8, 128))
    gain2 = jnp.concatenate([gain_ref[...], gain_ref[...]], axis=1)
    gain4 = jnp.concatenate([gain2, gain2], axis=1)
    row_block = lax.broadcasted_iota(jnp.int32, (4 * CH, 4 * CH), 0) // CH
    col_block = lax.broadcasted_iota(jnp.int32, (4 * CH, 4 * CH), 1) // CH
    diagonal = row_block == col_block
    wide = jnp.concatenate([mix_ref[...].astype(F32)] * 2, axis=1)
    wide = jnp.concatenate([wide, wide], axis=1)
    wide = jnp.concatenate([wide] * 4, axis=0)
    wdiag[0] = jnp.where(diagonal, wide, 0.0).astype(BF16)
    wdiag[1] = jnp.where(diagonal, 1.0 / CH, 0.0).astype(BF16)
    mixacc[...] = jnp.zeros_like(mixacc)
    gainacc[...] = jnp.zeros_like(gainacc)

    load_feat.wait()
    fill_own(feat, field, low)
    gather_edges(field, ysend, csend)

    def halo_copies(src, ys, cs, xr, yr, cr, send, land):
        copies = []
        for step in (-1, 1):
            far = (step + 1) // 2
            copies.append((src.at[far * (SIDE - 1)], xr.at[1 - far], (peer_x(step), gy)))
            copies.append((ys.at[far], yr.at[1 - far], (gx, peer_y(step))))
        for dx in (-1, 1):
            for dy in (-1, 1):
                here = (dx + 1) + (dy + 1) // 2
                copies.append((cs.at[here], cr.at[3 - here], (peer_x(dx), peer_y(dy))))
        return [
            pltpu.make_async_remote_copy(
                src_ref=a, dst_ref=b, send_sem=send.at[n], recv_sem=land.at[n],
                device_id=to, device_id_type=MESH,
            )
            for n, (a, b, to) in enumerate(copies)
        ]

    pl.semaphore_wait(barrier, (n_gx - 1) + (n_gy - 1) + 4)
    halo1 = halo_copies(feat, ysend, csend, xrecv1, yrecv1, crecv1, send1, land1)
    for copy in halo1:
        copy.start()
    for copy in halo1:
        copy.wait()
    fill_halo(field, xrecv1, yrecv1, crecv1, masks, low)

    weights = [tapsb[8 * tap : 8 * tap + 8, :] for tap in range(27)]
    stencil(field, weights, depth)

    load_cot.wait()
    cells = SIDE * SIDE

    @pl.loop(0, KT // 2)
    def _(m):
        lanes = pl.ds(pl.multiple_of(m * 256, 256), 256)
        values = jnp.concatenate(
            [depth[:, 2 * m + h].reshape(cells, 128) for h in range(2)], axis=1
        )
        mean_square = jnp.dot((values * values).astype(BF16), wdiag[1], preferred_element_type=F32)
        inv_rms = lax.rsqrt(mean_square + EPS)
        normed = values * inv_rms
        norm_bf = (normed * gain4).astype(BF16)
        branch = jnp.dot(norm_bf, wdiag[0], preferred_element_type=F32)
        inputs = feat[:, :, lanes].reshape(cells, 256).astype(F32)
        mixed[:, :, lanes] = (inputs + branch).astype(BF16).reshape(SIDE, SIDE, 256)
        grad_out = cot[:, :, lanes].reshape(cells, 256)
        grad_norm = lax.dot_general(
            grad_out, wdiag[0], (((1,), (1,)), ((), ())), preferred_element_type=F32
        )
        product = grad_norm * normed
        gainacc[...] += jnp.sum(product.reshape(cells // 8, 8, 256), axis=0)
        mean = jnp.dot((product * gain4).astype(BF16), wdiag[1], preferred_element_type=F32)
        grad_depth = inv_rms * (grad_norm * gain4 - normed * mean)
        gd[:, :, lanes] = grad_depth.astype(BF16).reshape(SIDE, SIDE, 256)
        mixacc[...] += lax.dot_general(
            norm_bf, grad_out, (((0,), (0,)), ((), ())), preferred_element_type=F32
        )

    fill_own(gd, gfield, low)
    gather_edges(gfield, ysend2, csend2)
    halo2 = halo_copies(gd, ysend2, csend2, xrecv2, yrecv2, crecv2, send2, land2)
    for copy in halo2:
        copy.start()

    totals = list(tap_products(field, gfield))
    totals.append(gainacc[:, :128] + gainacc[:, 128:])
    folded = [total + pltpu.roll(total, CH, 1) for total in totals]
    for j in range(14):
        pair = jnp.where(low8, folded[2 * j], folded[2 * j + 1])
        pbuf[j : j + 1, :] = jnp.sum(pair, axis=0, keepdims=True)
    pbuf[14:16, :] = jnp.zeros((2, 128), F32)
    even = mixacc[0:CH, 0:128] + mixacc[2 * CH : 3 * CH, 128:256]
    odd = mixacc[CH : 2 * CH, 0:128] + mixacc[3 * CH : 4 * CH, 128:256]
    wide_low = lax.broadcasted_iota(jnp.int32, (CH, 128), 1) < CH
    both = jnp.where(wide_low, even, odd)
    both = both + pltpu.roll(both, CH, 1)
    pbuf[16:48, :] = jnp.where(wide_low[:32], both[:32], both[32:])

    per_peer = 48 // n_gx
    red[...] = jnp.zeros_like(red)
    for q in range(per_peer):
        red[:, q, :] = pbuf[n_gx * q : n_gx * q + n_gx, :]

    def remote(src, dst, index, to):
        return pltpu.make_async_remote_copy(
            src_ref=src, dst_ref=dst, send_sem=rsend.at[index], recv_sem=rland.at[index],
            device_id=to, device_id_type=MESH,
        )

    def landed(buffer, index):
        pltpu.make_async_copy(buffer, buffer, rland.at[index]).wait()

    @pl.loop(1, n_gx)
    def _(d):
        remote(red.at[peer_x(d)], recv1.at[d - 1], 0, (peer_x(d), gy)).start()

    landed(recv1, 0)
    part2[...] = red[gx] + jnp.sum(recv1[...], axis=0)
    recv2[gy] = part2[...]

    @pl.loop(1, n_gy)
    def _(d):
        remote(part2, recv2.at[gy], 1, (gx, peer_y(d))).start()

    for copy in halo2:
        copy.wait()
    fill_halo(gfield, xrecv2, yrecv2, crecv2, masks, low)

    def finish(k):
        lanes = pl.ds(pl.multiple_of(k * 128, 128), 128)
        for x in range(SIDE):
            total = cot[x, :, lanes].astype(F32) + depth[x, k]
            gf[x, :, lanes] = total.astype(BF16)

    stencil(gfield, weights[::-1], depth, finish)

    landed(recv2.at[pl.ds(0, n_gy - 1)], 1)
    part3[...] = jnp.sum(recv2[...], axis=0)
    gath[gx] = part3[...]

    @pl.loop(1, n_gx)
    def _(d):
        remote(part3, gath.at[gx], 2, (peer_x(d), gy)).start()

    landed(gath.at[pl.ds(0, n_gx - 1)], 2)
    for q in range(per_peer):
        pbuf[n_gx * q : n_gx * q + n_gx, :] = gath[:, q, :]
    def sent(buffer, index):
        pltpu.make_async_copy(buffer, buffer, rsend.at[index]).wait()

    sent(recv1, 0)
    sent(recv2.at[pl.ds(0, n_gy - 1)], 1)
    sent(gath.at[pl.ds(0, n_gx - 1)], 2)


def deliver(
    mixed, gf, pbuf, mixed_hbm, gf_hbm, gt_hbm, gg_hbm, gm_hbm, gt_ref, gg_ref, gm_ref, sem
):
    copies = [
        pltpu.make_async_copy(src, dst, sem.at[n])
        for n, (src, dst) in enumerate(
            (
                (mixed, mixed_hbm), (gf, gf_hbm),
                (gt_ref, gt_hbm), (gg_ref, gg_hbm), (gm_ref, gm_hbm),
            )
        )
    ]
    copies[0].start()
    copies[1].start()
    rows = pbuf[0:16, :]
    turned = pltpu.roll(rows, CH, 1)
    for tap in range(27):
        source = turned if tap % 2 else rows
        gt_ref[tap : tap + 1, :] = source[tap // 2 : tap // 2 + 1, :CH]
    gg_ref[...] = turned[13:14, :CH]
    packed = pbuf[16:48, :]
    gm_ref[0:32, :] = packed[:, :CH]
    gm_ref[32:64, :] = pltpu.roll(packed, CH, 1)[:, :CH]

    for copy in copies[2:]:
        copy.start()
    for copy in copies:
        copy.wait()


def shards(n_gx, n_gy, features, slot_map, tap_weights, gain, mix_weight, cotangent):
    block = (SIDE, SIDE, LANES)
    padded = max(4, 48 // n_gx)
    vmem = pl.BlockSpec(memory_space=pltpu.VMEM)
    hbm = pl.BlockSpec(memory_space=pltpu.HBM)
    smem = pl.BlockSpec(memory_space=pltpu.SMEM)
    halo = [
        pltpu.VMEM((2, SIDE, LANES), BF16),
        pltpu.VMEM((2, SIDE, LANES), BF16),
        pltpu.VMEM((4, KT, 128), F32),
    ]
    mixed, grad_features, sums = pl.pallas_call(
        functools.partial(kernel, n_gx, n_gy),
        out_shape=(
            jax.ShapeDtypeStruct(block, BF16),
            jax.ShapeDtypeStruct(block, BF16),
            jax.ShapeDtypeStruct((48, 128), F32),
        ),
        in_specs=[hbm, smem, hbm, hbm, hbm, hbm],
        out_specs=(vmem, vmem, vmem),
        scratch_shapes=[
            pltpu.VMEM((27, CH), F32), pltpu.VMEM((1, CH), F32), pltpu.VMEM((CH, CH), BF16)
        ]
        + [pltpu.VMEM(block, BF16)] * 3
        + [pltpu.VMEM((3 * FIELD, 128), F32)] * 2
        + [
            pltpu.VMEM((SIDE, KT, SIDE, 128), F32),
            pltpu.VMEM((27 * 8, 128), F32),
            pltpu.VMEM((2, 4 * CH, 4 * CH), BF16),
            pltpu.VMEM((4 * CH, 4 * CH), F32),
            pltpu.VMEM((8, 4 * CH), F32),
        ]
        + halo
        + halo
        + halo[1:]
        + halo[1:]
        + [
            pltpu.VMEM((n_gx, padded, 128), F32),
            pltpu.VMEM((n_gx - 1, padded, 128), F32),
            pltpu.VMEM((padded, 128), F32),
            pltpu.VMEM((n_gy, padded, 128), F32),
            pltpu.VMEM((padded, 128), F32),
            pltpu.VMEM((n_gx, padded, 128), F32),
            pltpu.SemaphoreType.DMA((5,)),
            pltpu.SemaphoreType.DMA((8,)),
            pltpu.SemaphoreType.DMA((8,)),
            pltpu.SemaphoreType.DMA((8,)),
            pltpu.SemaphoreType.DMA((8,)),
            pltpu.SemaphoreType.DMA((3,)),
            pltpu.SemaphoreType.DMA((3,)),
        ],
        compiler_params=pltpu.CompilerParams(
            collective_id=0, has_side_effects=True, vmem_limit_bytes=40 * 1024 * 1024
        ),
        name="block_conv",
    )(
        *(
            pltpu.with_memory_space_constraint(value, pltpu.HBM)
            for value in (
                features.reshape(block), slot_map.transpose(0, 2, 1), tap_weights,
                gain.reshape(1, CH), mix_weight, cotangent.reshape(block),
            )
        )
    )
    mixed, grad_features, grad_taps, grad_gain, grad_mix = pl.pallas_call(
        deliver,
        out_shape=(
            jax.ShapeDtypeStruct(block, BF16),
            jax.ShapeDtypeStruct(block, BF16),
            jax.ShapeDtypeStruct((27, CH), F32),
            jax.ShapeDtypeStruct((1, CH), F32),
            jax.ShapeDtypeStruct((CH, CH), F32),
        ),
        in_specs=[vmem] * 3,
        out_specs=(hbm,) * 5,
        scratch_shapes=[
            pltpu.VMEM((27, CH), F32), pltpu.VMEM((1, CH), F32), pltpu.VMEM((CH, CH), F32),
            pltpu.SemaphoreType.DMA((5,)),
        ],
        compiler_params=pltpu.CompilerParams(vmem_limit_bytes=4 * 1024 * 1024),
        name="deliver",
    )(mixed, grad_features, sums)
    return (
        mixed.reshape(features.shape), grad_features.reshape(features.shape),
        grad_taps, grad_gain.reshape(CH), grad_mix,
    )


def solution(mesh):
    return jax.shard_map(
        functools.partial(shards, mesh.shape["gx"], mesh.shape["gy"]),
        mesh=mesh,
        in_specs=(P("gx", "gy", None, None), P(), P(), P(), P(), P("gx", "gy", None, None)),
        out_specs=(P("gx", "gy", None, None), P("gx", "gy", None, None), P(), P(), P()),
        check_vma=False,
    )
```

```python
import functools

import jax
import jax.numpy as jnp
from jax import lax
from jax.experimental import pallas as pl
from jax.experimental.pallas import tpu as pltpu
from jax.sharding import PartitionSpec as P

EPS = 1e-05
MESH = pl.DeviceIdType.MESH
F32 = jnp.float32
BF16 = jnp.bfloat16
SIDE = 16
CH = 64
KT = 8
LANES = KT * 128
ROWS = 32
SLOT = KT * ROWS
FIELD = (SIDE + 2) * SLOT
Y0 = 8
CELLS = SIDE * SIDE
OFFSETS = (-1, 0, 1)


def zrow(oz, slot, tile):
    return oz * FIELD + slot * SLOT + tile * ROWS


def shifted_tiles(tiles, low):
    count = len(tiles)
    rot = [pltpu.roll(tile, CH, 1) for tile in tiles]
    down = [jnp.where(low, rot[k - 1], rot[k]) for k in range(count)]
    up = [jnp.where(low, rot[k], rot[(k + 1) % count]) for k in range(count)]
    return down, up


def fill_own(tile_of, field, low):
    @pl.loop(0, SIDE, step=2)
    def _(first):
        for x in (first, first + 1):
            tiles = [tile_of(x, k) for k in range(KT)]
            down, up = shifted_tiles(tiles, low)
            down[0] = jnp.where(low, 0.0, down[0])
            up[-1] = jnp.where(low, up[-1], 0.0)
            for oz, values in enumerate((down, tiles, up)):
                rows = field.at[pl.ds(pl.multiple_of(oz * FIELD + (x + 1) * SLOT, SLOT), SLOT)]
                for k in range(KT):
                    rows[k * ROWS + Y0 : k * ROWS + Y0 + SIDE, :] = values[k]


def zero_halo(field, ycols):
    zero = jnp.zeros((8, 128), F32)
    for oz in range(3):
        for slot in (0, SIDE + 1):
            field[zrow(oz, slot, 0) : zrow(oz, slot, 0) + SLOT, :] = jnp.zeros((SLOT, 128), F32)

    @pl.loop(0, SIDE)
    def _(x):
        for oz in range(3):
            rows = field.at[pl.ds(pl.multiple_of(oz * FIELD + (x + 1) * SLOT, SLOT), SLOT)]
            for k in range(KT):
                rows[k * ROWS : k * ROWS + 8, :] = zero
                rows[k * ROWS + 24 : k * ROWS + 32, :] = zero

    @pl.loop(0, 6 * KT)
    def _(group):
        rows = ycols.at[pl.ds(pl.multiple_of(group * ROWS, ROWS), ROWS)]
        rows[0:8, :] = zero
        rows[24:32, :] = zero


def gather_edges(column, corner, ysend, csend):
    for side in range(2):
        for k in range(KT):
            values = column(k, side * (SIDE - 1))
            ysend[side, :, k * 128 : (k + 1) * 128] = values.astype(BF16)
    for hx in range(2):
        for hy in range(2):
            csend[2 * hx + hy] = corner(hx * (SIDE - 1), hy * (SIDE - 1))


def fill_halo(field, xrecv, yrecv, crecv, masks, low, ycols=None):
    def masked(tiles, mask):
        same, below, above = mask
        down, up = shifted_tiles(tiles, low)
        first = jnp.where(low, below, same)
        last = jnp.where(low, same, above)
        down = [v * (first if k == 0 else same) for k, v in enumerate(down)]
        up = [v * (last if k == KT - 1 else same) for k, v in enumerate(up)]
        return down, [v * same for v in tiles], up

    for side in range(2):
        tiles = [xrecv[side, :, k * 128 : (k + 1) * 128].astype(F32) for k in range(KT)]
        for oz, values in enumerate(masked(tiles, masks[(2 * side - 1, 0)])):
            for k in range(KT):
                start = zrow(oz, side * (SIDE + 1), k) + Y0
                field[start : start + SIDE, :] = values[k]
        tiles = [yrecv[side, :, k * 128 : (k + 1) * 128].astype(F32) for k in range(KT)]
        for oz, values in enumerate(masked(tiles, masks[(0, 2 * side - 1)])):
            for k in range(KT):
                start = zrow(oz, 1, k) + (Y0 - 1, Y0 + SIDE)[side]
                field[pl.ds(start, SIDE, stride=SLOT), :] = values[k]
                if ycols is not None:
                    start = ((side * 3 + oz) * KT + k) * ROWS + Y0
                    ycols[start : start + SIDE, :] = values[k]
    low8 = low[:KT]
    row8 = lax.broadcasted_iota(jnp.int32, (KT, 128), 0)
    for hx in range(2):
        for hy in range(2):
            same, below, above = masks[(2 * hx - 1, 2 * hy - 1)]
            cell = crecv[2 * hx + hy]
            rot = pltpu.roll(cell, CH, 1)
            down = jnp.where(low8, pltpu.roll(rot, 1, 0), rot)
            up = jnp.where(low8, rot, pltpu.roll(rot, KT - 1, 0))
            down = down * jnp.where(low8 & (row8 == 0), below, same)
            up = up * jnp.where((~low8) & (row8 == KT - 1), above, same)
            for oz, value in enumerate((down, cell * same, up)):
                start = zrow(oz, hx * (SIDE + 1), 0) + (Y0 - 1, Y0 + SIDE)[hy]
                field[pl.ds(start, KT, stride=ROWS), :] = value


def tap_index(ox, oy, oz):
    return 9 * (ox + 1) + 3 * (oy + 1) + oz + 1


def stencil(field, weights, result, first, last, finish=None):
    @pl.loop(first, last)
    def _(k):
        rows = field.at[pl.ds(pl.multiple_of(k * ROWS, ROWS), 3 * FIELD - (KT - 1) * ROWS)]
        out = result.at[pl.ds(pl.multiple_of(k * CELLS, CELLS), CELLS)]
        for half in range(2):
            sums = {}
            for slot in range(SIDE + 2):
                for oz in OFFSETS:
                    for oy in OFFSETS:
                        start = (oz + 1) * FIELD + slot * SLOT + Y0 + 8 * half + oy
                        value = rows[start : start + 8, :]
                        for ox in OFFSETS:
                            x = slot - 1 - ox
                            if 0 <= x < SIDE:
                                term = value * weights[tap_index(ox, oy, oz)]
                                sums[x] = sums[x] + term if x in sums else term
                if slot >= 2:
                    start = (slot - 2) * SIDE + 8 * half
                    out[start : start + 8, :] = sums.pop(slot - 2)
        if finish is not None:
            finish(k, out)


def add_halo_terms(field, ycols, weights, result):
    @pl.loop(0, KT)
    def _(k):
        rows = field.at[pl.ds(pl.multiple_of(k * ROWS, ROWS), 3 * FIELD - (KT - 1) * ROWS)]
        cols = ycols.at[pl.ds(pl.multiple_of(k * ROWS, ROWS), (5 * KT + 1) * ROWS)]
        out = result.at[pl.ds(pl.multiple_of(k * CELLS, CELLS), CELLS)]
        for side in range(2):
            step = 2 * side - 1
            for half in range(2):
                start = side * (SIDE - 1) * SIDE + 8 * half
                total = out[start : start + 8, :]
                for oz in OFFSETS:
                    for oy in OFFSETS:
                        at = (oz + 1) * FIELD + side * (SIDE + 1) * SLOT + Y0 + 8 * half + oy
                        total += rows[at : at + 8, :] * weights[tap_index(step, oy, oz)]
                out[start : start + 8, :] = total
        for side in range(2):
            step = 2 * side - 1
            for half in range(2):
                span = pl.ds(8 * half * SIDE + side * (SIDE - 1), 8, stride=SIDE)
                total = out[span, :]
                for oz in OFFSETS:
                    for ox in OFFSETS:
                        at = (side * 3 + oz + 1) * KT * ROWS + Y0 + 8 * half + ox
                        total += cols[at : at + 8, :] * weights[tap_index(ox, step, oz)]
                out[span, :] = total


def tap_products(field, grads, taps):
    def body(k, totals):
        totals = dict(zip(taps, totals))
        rows = field.at[pl.ds(pl.multiple_of(k * ROWS, ROWS), 3 * FIELD - (KT - 1) * ROWS)]
        own = grads.at[pl.ds(pl.multiple_of(k * CELLS, CELLS), CELLS)]
        for half in range(2):
            for slot in range(SIDE + 2):
                near = {}
                for ox in OFFSETS:
                    x = slot - 1 - ox
                    if 0 <= x < SIDE:
                        start = x * SIDE + 8 * half
                        near[ox] = own[start : start + 8, :]
                for oz in OFFSETS:
                    for oy in OFFSETS:
                        wanted = [ox for ox in near if (ox, oy, oz) in totals]
                        if not wanted:
                            continue
                        start = (oz + 1) * FIELD + slot * SLOT + Y0 + 8 * half + oy
                        value = rows[start : start + 8, :]
                        for ox in wanted:
                            totals[(ox, oy, oz)] = totals[(ox, oy, oz)] + value * near[ox]
        return tuple(totals[tap] for tap in taps)

    zero = jnp.zeros((8, 128), F32)
    return list(lax.fori_loop(0, KT, body, (zero,) * len(taps)))


TAPS = [(ox, oy, oz) for oz in OFFSETS for oy in OFFSETS for ox in OFFSETS]
GROUPS = (TAPS[:16], TAPS[16:])


def kernel(
    n_gx, n_gy,
    feat_hbm, map_ref, taps_hbm, gain_hbm, mix_hbm, cot_hbm,
    mixed, gf, tap_sums, mix_sums,
    taps_ref, gain_ref, mix_ref, feat, cot,
    field, gfield, depth, grads, ycols, normb, gnorm, xsend2, tapsb, wdiag, mixacc, gainacc,
    xrecv1, yrecv1, crecv1, xrecv2, yrecv2, crecv2, ysend, csend, ysend2, csend2,
    red, recv1, part2, recv2, part3, gath, tsend, trecv1, tpart, trecv2,
    io_sem, send1, land1, send2, land2, rsend, rland,
):
    gx = lax.axis_index("gx")
    gy = lax.axis_index("gy")

    load_feat = pltpu.make_async_copy(feat_hbm, feat, io_sem.at[0])
    load_cot = pltpu.make_async_copy(cot_hbm, cot, io_sem.at[1])
    load_params = [
        pltpu.make_async_copy(src, dst, io_sem.at[2 + n])
        for n, (src, dst) in enumerate(
            ((taps_hbm, taps_ref), (gain_hbm, gain_ref), (mix_hbm, mix_ref))
        )
    ]

    def peer_x(d):
        return lax.rem(gx + d + n_gx, n_gx)

    def peer_y(d):
        return lax.rem(gy + d + n_gy, n_gy)

    barrier = pltpu.get_barrier_semaphore()

    def greet(dx, dy):
        pl.semaphore_signal(
            barrier, inc=1, device_id=(peer_x(dx), peer_y(dy)), device_id_type=MESH
        )

    around = [(dx, dy) for dx in OFFSETS for dy in OFFSETS if (dx, dy) != (0, 0)]
    for dx, dy in around:
        greet(dx, dy)
    load_feat.start()
    for copy in load_params:
        copy.start()
    load_cot.start()

    @pl.loop(2, n_gx - 1)
    def _(d):
        greet(d, 0)

    @pl.loop(2, n_gy - 1)
    def _(d):
        greet(0, d)

    low = lax.broadcasted_iota(jnp.int32, (SIDE, 128), 1) < CH
    low8 = low[:8]

    def level(i, j):
        return jnp.where(map_ref[i, 1, j] == 0, 1, 0)

    own_level = level(gx, gy)
    masks = {}
    for dx, dy in around:
        inside = (gx + dx >= 0) & (gx + dx < n_gx) & (gy + dy >= 0) & (gy + dy < n_gy)
        delta = level(peer_x(dx), peer_y(dy)) - own_level
        masks[(dx, dy)] = tuple(
            jnp.where(inside & (delta == step), 1.0, 0.0).astype(F32) for step in (0, -1, 1)
        )

    load_feat.wait()
    fill_own(lambda x, k: feat[x, :, k * 128 : (k + 1) * 128].astype(F32), field, low)
    gather_edges(
        lambda k, y: field[pl.ds(zrow(1, 1, k) + Y0 + y, SIDE, stride=SLOT), :],
        lambda x, y: field[pl.ds(zrow(1, 1 + x, 0) + Y0 + y, KT, stride=ROWS), :],
        ysend, csend,
    )

    def halo_copies(src, ys, cs, xr, yr, cr, send, land):
        copies = []
        for far in range(2):
            step = 2 * far - 1
            copies.append((src(far), xr.at[1 - far], (peer_x(step), gy)))
            copies.append((ys.at[far], yr.at[1 - far], (gx, peer_y(step))))
        for dx in (-1, 1):
            for dy in (-1, 1):
                here = (dx + 1) + (dy + 1) // 2
                copies.append((cs.at[here], cr.at[3 - here], (peer_x(dx), peer_y(dy))))
        return [
            pltpu.make_async_remote_copy(
                src_ref=a, dst_ref=b, send_sem=send.at[n], recv_sem=land.at[n],
                device_id=to, device_id_type=MESH,
            )
            for n, (a, b, to) in enumerate(copies)
        ]

    pl.semaphore_wait(barrier, (n_gx - 1) + (n_gy - 1) + 4)
    halo1 = halo_copies(
        lambda far: feat.at[far * (SIDE - 1)], ysend, csend, xrecv1, yrecv1, crecv1, send1, land1
    )
    for copy in halo1:
        copy.start()

    for copy in load_params:
        copy.wait()
    taps2 = jnp.concatenate([taps_ref[...], taps_ref[...]], axis=1)
    for tap in range(27):
        tapsb[8 * tap : 8 * tap + 8, :] = jnp.broadcast_to(taps2[tap : tap + 1, :], (8, 128))
    gain2 = jnp.concatenate([gain_ref[...], gain_ref[...]], axis=1)
    gain4 = jnp.concatenate([gain2, gain2], axis=1)
    row_block = lax.broadcasted_iota(jnp.int32, (4 * CH, 4 * CH), 0) // CH
    col_block = lax.broadcasted_iota(jnp.int32, (4 * CH, 4 * CH), 1) // CH
    diagonal = row_block == col_block
    wide = jnp.concatenate([mix_ref[...].astype(F32)] * 2, axis=1)
    wide = jnp.concatenate([wide, wide], axis=1)
    wide = jnp.concatenate([wide] * 4, axis=0)
    wdiag[0] = jnp.where(diagonal, wide, 0.0).astype(BF16)
    wdiag[1] = jnp.where(diagonal, 1.0 / CH, 0.0).astype(BF16)
    mixacc[...] = jnp.zeros_like(mixacc)
    gainacc[...] = jnp.zeros_like(gainacc)
    zero_halo(field, ycols)
    weights = [tapsb[8 * tap : 8 * tap + 8, :] for tap in range(27)]
    stencil(field, weights, depth, 0, KT)
    load_cot.wait()

    def wide_lanes(m):
        return pl.ds(pl.multiple_of(m * 256, 256), 256)

    @pl.loop(0, KT // 2)
    def _(m):
        gnorm[m] = lax.dot_general(
            cot[:, :, wide_lanes(m)].reshape(CELLS, 256), wdiag[0],
            (((1,), (1,)), ((), ())), preferred_element_type=F32,
        )

    for copy in halo1:
        copy.wait_recv()
    fill_halo(field, xrecv1, yrecv1, crecv1, masks, low, ycols)
    add_halo_terms(field, ycols, weights, depth)

    @pl.loop(0, KT // 2)
    def _(m):
        lanes = wide_lanes(m)
        tiles = [pl.ds(pl.multiple_of((2 * m + h) * CELLS, CELLS), CELLS) for h in range(2)]
        values = jnp.concatenate([depth[tile, :] for tile in tiles], axis=1)
        mean_square = jnp.dot((values * values).astype(BF16), wdiag[1], preferred_element_type=F32)
        inv_rms = lax.rsqrt(mean_square + EPS)
        normed = values * inv_rms
        norm_bf = (normed * gain4).astype(BF16)
        normb[:, lanes] = norm_bf
        grad_norm = gnorm[m]
        product = grad_norm * normed
        gainacc[...] += jnp.sum(product.reshape(CELLS // 8, 8, 256), axis=0)
        mean = jnp.dot((product * gain4).astype(BF16), wdiag[1], preferred_element_type=F32)
        grad_depth = (inv_rms * (grad_norm * gain4 - normed * mean)).astype(BF16)
        for far in range(2):
            start = far * SIDE * (SIDE - 1)
            xsend2[far, :, lanes] = grad_depth[start : start + SIDE]
        for h, tile in enumerate(tiles):
            grads[tile, :] = grad_depth[:, h * 128 : (h + 1) * 128].astype(F32)
        mixacc[...] += lax.dot_general(
            norm_bf, cot[:, :, lanes].reshape(CELLS, 256),
            (((0,), (0,)), ((), ())), preferred_element_type=F32,
        )

    even = mixacc[0:CH, 0:128] + mixacc[2 * CH : 3 * CH, 128:256]
    odd = mixacc[CH : 2 * CH, 0:128] + mixacc[3 * CH : 4 * CH, 128:256]
    wide_low = lax.broadcasted_iota(jnp.int32, (CH, 128), 1) < CH
    both = jnp.where(wide_low, even, odd)
    both = both + pltpu.roll(both, CH, 1)
    packed = jnp.where(wide_low[:32], both[:32], both[32:])
    per_peer = 32 // n_gx
    for q in range(per_peer):
        red[:, q, :] = packed[n_gx * q : n_gx * q + n_gx, :]

    def remote(src, dst, index, to):
        return pltpu.make_async_remote_copy(
            src_ref=src, dst_ref=dst, send_sem=rsend.at[index], recv_sem=rland.at[index],
            device_id=to, device_id_type=MESH,
        )

    def landed(buffer, index):
        pltpu.make_async_copy(buffer, buffer, rland.at[index]).wait()

    @pl.loop(1, n_gx)
    def _(d):
        remote(red.at[peer_x(d)], recv1.at[d - 1], 0, (peer_x(d), gy)).start()

    gather_edges(
        lambda k, y: grads[pl.ds(k * CELLS + y, SIDE, stride=SIDE), :],
        lambda x, y: grads[pl.ds(x * SIDE + y, KT, stride=CELLS), :],
        ysend2, csend2,
    )
    halo2 = halo_copies(
        lambda far: xsend2.at[far], ysend2, csend2, xrecv2, yrecv2, crecv2, send2, land2
    )
    for copy in halo2:
        copy.start()

    for group, taps in enumerate(GROUPS):
        totals = tap_products(field, grads, taps)
        if group == 1:
            totals.append(gainacc[:, :128] + gainacc[:, 128:])
        for j in range(len(totals) // 2):
            pair = jnp.where(
                low8,
                totals[2 * j] + pltpu.roll(totals[2 * j], CH, 1),
                totals[2 * j + 1] + pltpu.roll(totals[2 * j + 1], CH, 1),
            )
            tsend[group, j : j + 1, :] = jnp.sum(pair, axis=0, keepdims=True)
        if group == 1:
            tsend[1, 6:8, :] = jnp.zeros((2, 128), F32)
        trecv1[group, gx] = tsend[group]

        @pl.loop(1, n_gx)
        def _(d):
            remote(tsend.at[group], trecv1.at[group, gx], 3 + group, (peer_x(d), gy)).start()

    fill_own(
        lambda x, k: grads[pl.ds(pl.multiple_of(k * CELLS + x * SIDE, SIDE), SIDE), :],
        gfield, low,
    )

    @pl.loop(0, KT // 2)
    def _(m):
        lanes = wide_lanes(m)
        branch = jnp.dot(normb[:, lanes], wdiag[0], preferred_element_type=F32)
        inputs = feat[:, :, lanes].reshape(CELLS, 256).astype(F32)
        mixed[:, :, lanes] = (inputs + branch).astype(BF16).reshape(SIDE, SIDE, 256)

    landed(recv1, 0)
    part2[...] = red[gx] + jnp.sum(recv1[...], axis=0)
    recv2[gy] = part2[...]

    @pl.loop(1, n_gy)
    def _(d):
        remote(part2, recv2.at[gy], 1, (gx, peer_y(d))).start()

    for copy in halo2:
        copy.wait_recv()
    fill_halo(gfield, xrecv2, yrecv2, crecv2, masks, low)

    def finish(k, out):
        lanes = pl.ds(pl.multiple_of(k * 128, 128), 128)
        for x in range(SIDE):
            total = cot[x, :, lanes].astype(F32) + out[x * SIDE : (x + 1) * SIDE, :]
            gf[x, :, lanes] = total.astype(BF16)

    stencil(gfield, weights[::-1], depth, 0, KT // 2, finish)
    for group in range(2):
        landed(trecv1.at[group, pl.ds(0, n_gx - 1)], 3 + group)
        tpart[group] = jnp.sum(trecv1[group], axis=0)
        trecv2[group, gy] = tpart[group]

        @pl.loop(1, n_gy)
        def _(d):
            remote(tpart.at[group], trecv2.at[group, gy], 5 + group, (gx, peer_y(d))).start()

    stencil(gfield, weights[::-1], depth, KT // 2, KT, finish)
    landed(recv2.at[pl.ds(0, n_gy - 1)], 1)
    part3[...] = jnp.sum(recv2[...], axis=0)
    gath[gx] = part3[...]

    @pl.loop(1, n_gx)
    def _(d):
        remote(part3, gath.at[gx], 2, (peer_x(d), gy)).start()

    def sent(buffer, index):
        pltpu.make_async_copy(buffer, buffer, rsend.at[index]).wait()

    for copy in halo1 + halo2:
        copy.wait_send()
    sent(recv1, 0)
    sent(recv2.at[pl.ds(0, n_gy - 1)], 1)
    for group in range(2):
        sent(trecv1.at[group, pl.ds(0, n_gx - 1)], 3 + group)
        landed(trecv2.at[group, pl.ds(0, n_gy - 1)], 5 + group)
        tap_sums[group] = jnp.sum(trecv2[group], axis=0)
        sent(trecv2.at[group, pl.ds(0, n_gy - 1)], 5 + group)
    landed(gath.at[pl.ds(0, n_gx - 1)], 2)
    for q in range(per_peer):
        mix_sums[n_gx * q : n_gx * q + n_gx, :] = gath[:, q, :]
    sent(gath.at[pl.ds(0, n_gx - 1)], 2)


def deliver(
    mixed, gf, tap_sums, mix_sums, mixed_hbm, gf_hbm, gt_hbm, gg_hbm, gm_hbm,
    gt_ref, gg_ref, gm_ref, sem,
):
    copies = [
        pltpu.make_async_copy(src, dst, sem.at[n])
        for n, (src, dst) in enumerate(
            (
                (mixed, mixed_hbm), (gf, gf_hbm),
                (gt_ref, gt_hbm), (gg_ref, gg_hbm), (gm_ref, gm_hbm),
            )
        )
    ]
    copies[0].start()
    copies[1].start()
    for group, taps in enumerate(GROUPS):
        rows = tap_sums[group]
        turned = pltpu.roll(rows, CH, 1)
        for place, tap in enumerate(taps):
            source = turned if place % 2 else rows
            row = tap_index(*tap)
            gt_ref[row : row + 1, :] = source[place // 2 : place // 2 + 1, :CH]
        if group == 1:
            gg_ref[...] = turned[5:6, :CH]
    gm_ref[0:32, :] = mix_sums[:, :CH]
    gm_ref[32:64, :] = pltpu.roll(mix_sums[...], CH, 1)[:, :CH]
    for copy in copies[2:]:
        copy.start()
    for copy in copies:
        copy.wait()


def shards(n_gx, n_gy, features, slot_map, tap_weights, gain, mix_weight, cotangent):
    block = (SIDE, SIDE, LANES)
    vmem = pl.BlockSpec(memory_space=pltpu.VMEM)
    hbm = pl.BlockSpec(memory_space=pltpu.HBM)
    smem = pl.BlockSpec(memory_space=pltpu.SMEM)
    halo = [
        pltpu.VMEM((2, SIDE, LANES), BF16),
        pltpu.VMEM((2, SIDE, LANES), BF16),
        pltpu.VMEM((4, KT, 128), F32),
    ]
    sums = (jax.ShapeDtypeStruct((2, 8, 128), F32), jax.ShapeDtypeStruct((32, 128), F32))
    share = 32 // n_gx
    mixed, grad_features, tap_sums, mix_sums = pl.pallas_call(
        functools.partial(kernel, n_gx, n_gy),
        out_shape=(
            jax.ShapeDtypeStruct(block, BF16), jax.ShapeDtypeStruct(block, BF16), *sums
        ),
        in_specs=[hbm, smem, hbm, hbm, hbm, hbm],
        out_specs=(vmem,) * 4,
        scratch_shapes=[
            pltpu.VMEM((27, CH), F32), pltpu.VMEM((1, CH), F32), pltpu.VMEM((CH, CH), BF16),
            pltpu.VMEM(block, BF16),
            pltpu.VMEM(block, BF16),
            pltpu.VMEM((3 * FIELD, 128), F32),
            pltpu.VMEM((3 * FIELD, 128), F32),
            pltpu.VMEM((KT * CELLS, 128), F32),
            pltpu.VMEM((KT * CELLS, 128), F32),
            pltpu.VMEM((6 * KT * ROWS, 128), F32),
            pltpu.VMEM((CELLS, LANES), BF16),
            pltpu.VMEM((4, CELLS, 256), F32),
            pltpu.VMEM((2, SIDE, LANES), BF16),
            pltpu.VMEM((27 * 8, 128), F32),
            pltpu.VMEM((2, 4 * CH, 4 * CH), BF16),
            pltpu.VMEM((4 * CH, 4 * CH), F32),
            pltpu.VMEM((8, 4 * CH), F32),
        ]
        + halo
        + halo
        + halo[1:]
        + halo[1:]
        + [
            pltpu.VMEM((n_gx, share, 128), F32),
            pltpu.VMEM((n_gx - 1, share, 128), F32),
            pltpu.VMEM((share, 128), F32),
            pltpu.VMEM((n_gy, share, 128), F32),
            pltpu.VMEM((share, 128), F32),
            pltpu.VMEM((n_gx, share, 128), F32),
            pltpu.VMEM((2, 8, 128), F32),
            pltpu.VMEM((2, n_gx, 8, 128), F32),
            pltpu.VMEM((2, 8, 128), F32),
            pltpu.VMEM((2, n_gy, 8, 128), F32),
            pltpu.SemaphoreType.DMA((5,)),
            pltpu.SemaphoreType.DMA((8,)),
            pltpu.SemaphoreType.DMA((8,)),
            pltpu.SemaphoreType.DMA((8,)),
            pltpu.SemaphoreType.DMA((8,)),
            pltpu.SemaphoreType.DMA((7,)),
            pltpu.SemaphoreType.DMA((7,)),
        ],
        compiler_params=pltpu.CompilerParams(
            collective_id=0, has_side_effects=True, vmem_limit_bytes=40 * 1024 * 1024
        ),
        name="block_conv",
    )(
        *(
            pltpu.with_memory_space_constraint(value, pltpu.HBM)
            for value in (
                features.reshape(block), slot_map.transpose(0, 2, 1), tap_weights,
                gain.reshape(1, CH), mix_weight, cotangent.reshape(block),
            )
        )
    )
    mixed, grad_features, grad_taps, grad_gain, grad_mix = pl.pallas_call(
        deliver,
        out_shape=(
            jax.ShapeDtypeStruct(block, BF16),
            jax.ShapeDtypeStruct(block, BF16),
            jax.ShapeDtypeStruct((27, CH), F32),
            jax.ShapeDtypeStruct((1, CH), F32),
            jax.ShapeDtypeStruct((CH, CH), F32),
        ),
        in_specs=[vmem] * 4,
        out_specs=(hbm,) * 5,
        scratch_shapes=[
            pltpu.VMEM((27, CH), F32), pltpu.VMEM((1, CH), F32), pltpu.VMEM((CH, CH), F32),
            pltpu.SemaphoreType.DMA((5,)),
        ],
        compiler_params=pltpu.CompilerParams(vmem_limit_bytes=4 * 1024 * 1024),
        name="deliver",
    )(mixed, grad_features, tap_sums, mix_sums)
    return (
        mixed.reshape(features.shape), grad_features.reshape(features.shape),
        grad_taps, grad_gain.reshape(CH), grad_mix,
    )


def solution(mesh):
    return jax.shard_map(
        functools.partial(shards, mesh.shape["gx"], mesh.shape["gy"]),
        mesh=mesh,
        in_specs=(P("gx", "gy", None, None), P(), P(), P(), P(), P("gx", "gy", None, None)),
        out_specs=(P("gx", "gy", None, None), P("gx", "gy", None, None), P(), P(), P()),
        check_vma=False,
    )
```

```python
import functools

import jax
import jax.numpy as jnp
from jax import lax
from jax.experimental import pallas as pl
from jax.experimental.pallas import tpu as pltpu
from jax.sharding import PartitionSpec as P

EPS = 1e-05
MESH = pl.DeviceIdType.MESH
F32 = jnp.float32
BF16 = jnp.bfloat16
SIDE = 16
CH = 64
KT = 8
LANES = KT * 128
ROWS = 32
SLOT = KT * ROWS
FIELD = (SIDE + 2) * SLOT
Y0 = 8
CELLS = SIDE * SIDE
OFFSETS = (-1, 0, 1)


def zrow(oz, slot, tile):
    return oz * FIELD + slot * SLOT + tile * ROWS


def shifted_tiles(tiles, low):
    count = len(tiles)
    rot = [pltpu.roll(tile, CH, 1) for tile in tiles]
    down = [jnp.where(low, rot[k - 1], rot[k]) for k in range(count)]
    up = [jnp.where(low, rot[k], rot[(k + 1) % count]) for k in range(count)]
    return down, up


def fill_own(tile_of, field, low):
    @pl.loop(0, SIDE, step=2)
    def _(first):
        for x in (first, first + 1):
            tiles = [tile_of(x, k) for k in range(KT)]
            down, up = shifted_tiles(tiles, low)
            down[0] = jnp.where(low, 0.0, down[0])
            up[-1] = jnp.where(low, up[-1], 0.0)
            for oz, values in enumerate((down, tiles, up)):
                rows = field.at[pl.ds(pl.multiple_of(oz * FIELD + (x + 1) * SLOT, SLOT), SLOT)]
                for k in range(KT):
                    rows[k * ROWS + Y0 : k * ROWS + Y0 + SIDE, :] = values[k]


def zero_halo(field, ycols):
    zero = jnp.zeros((8, 128), F32)
    for oz in range(3):
        for slot in (0, SIDE + 1):
            field[zrow(oz, slot, 0) : zrow(oz, slot, 0) + SLOT, :] = jnp.zeros((SLOT, 128), F32)

    @pl.loop(0, SIDE)
    def _(x):
        for oz in range(3):
            rows = field.at[pl.ds(pl.multiple_of(oz * FIELD + (x + 1) * SLOT, SLOT), SLOT)]
            for k in range(KT):
                rows[k * ROWS : k * ROWS + 8, :] = zero
                rows[k * ROWS + 24 : k * ROWS + 32, :] = zero

    @pl.loop(0, 6 * KT)
    def _(group):
        rows = ycols.at[pl.ds(pl.multiple_of(group * ROWS, ROWS), ROWS)]
        rows[0:8, :] = zero
        rows[24:32, :] = zero


def gather_edges(column, corner, ysend, csend):
    for side in range(2):
        for k in range(KT):
            values = column(k, side * (SIDE - 1))
            ysend[side, :, k * 128 : (k + 1) * 128] = values.astype(BF16)
    for hx in range(2):
        for hy in range(2):
            csend[2 * hx + hy] = corner(hx * (SIDE - 1), hy * (SIDE - 1))


def masked_shifts(tiles, mask, low):
    same, below, above = mask
    down, up = shifted_tiles(tiles, low)
    first = jnp.where(low, below, same)
    last = jnp.where(low, same, above)
    down = [v * (first if k == 0 else same) for k, v in enumerate(down)]
    up = [v * (last if k == KT - 1 else same) for k, v in enumerate(up)]
    return down, [v * same for v in tiles], up


def fill_x(field, xrecv, side, mask, low):
    tiles = [xrecv[side, :, k * 128 : (k + 1) * 128].astype(F32) for k in range(KT)]
    for oz, values in enumerate(masked_shifts(tiles, mask, low)):
        for k in range(KT):
            start = zrow(oz, side * (SIDE + 1), k) + Y0
            field[start : start + SIDE, :] = values[k]


def fill_y(field, yrecv, side, mask, low, ycols=None):
    tiles = [yrecv[side, :, k * 128 : (k + 1) * 128].astype(F32) for k in range(KT)]
    for oz, values in enumerate(masked_shifts(tiles, mask, low)):
        for k in range(KT):
            start = zrow(oz, 1, k) + (Y0 - 1, Y0 + SIDE)[side]
            field[pl.ds(start, SIDE, stride=SLOT), :] = values[k]
            if ycols is not None:
                start = ((side * 3 + oz) * KT + k) * ROWS + Y0
                ycols[start : start + SIDE, :] = values[k]


def fill_corner(field, crecv, hx, hy, mask, low):
    low8 = low[:KT]
    row8 = lax.broadcasted_iota(jnp.int32, (KT, 128), 0)
    same, below, above = mask
    cell = crecv[2 * hx + hy]
    rot = pltpu.roll(cell, CH, 1)
    down = jnp.where(low8, pltpu.roll(rot, 1, 0), rot)
    up = jnp.where(low8, rot, pltpu.roll(rot, KT - 1, 0))
    down = down * jnp.where(low8 & (row8 == 0), below, same)
    up = up * jnp.where((~low8) & (row8 == KT - 1), above, same)
    values = (down, cell * same, up)
    for oz, value in enumerate(values):
        start = zrow(oz, hx * (SIDE + 1), 0) + (Y0 - 1, Y0 + SIDE)[hy]
        field[pl.ds(start, KT, stride=ROWS), :] = value
    return values


def tap_index(ox, oy, oz):
    return 9 * (ox + 1) + 3 * (oy + 1) + oz + 1


def stencil(field, weights, result, first, last, finish=None):
    @pl.loop(first, last)
    def _(k):
        rows = field.at[pl.ds(pl.multiple_of(k * ROWS, ROWS), 3 * FIELD - (KT - 1) * ROWS)]
        out = result.at[pl.ds(pl.multiple_of(k * CELLS, CELLS), CELLS)]
        for half in range(2):
            sums = {}
            for slot in range(SIDE + 2):
                for oz in OFFSETS:
                    for oy in OFFSETS:
                        start = (oz + 1) * FIELD + slot * SLOT + Y0 + 8 * half + oy
                        value = rows[start : start + 8, :]
                        for ox in OFFSETS:
                            x = slot - 1 - ox
                            if 0 <= x < SIDE:
                                term = value * weights[tap_index(ox, oy, oz)]
                                sums[x] = sums[x] + term if x in sums else term
                if slot >= 2:
                    start = (slot - 2) * SIDE + 8 * half
                    out[start : start + 8, :] = sums.pop(slot - 2)
        if finish is not None:
            finish(k, out)


def add_x_terms(field, weights, result):
    @pl.loop(0, KT)
    def _(k):
        rows = field.at[pl.ds(pl.multiple_of(k * ROWS, ROWS), 3 * FIELD - (KT - 1) * ROWS)]
        out = result.at[pl.ds(pl.multiple_of(k * CELLS, CELLS), CELLS)]
        for side in range(2):
            step = 2 * side - 1
            for half in range(2):
                start = side * (SIDE - 1) * SIDE + 8 * half
                total = out[start : start + 8, :]
                for oz in OFFSETS:
                    for oy in OFFSETS:
                        at = (oz + 1) * FIELD + side * (SIDE + 1) * SLOT + Y0 + 8 * half + oy
                        total += rows[at : at + 8, :] * weights[tap_index(step, oy, oz)]
                out[start : start + 8, :] = total


def add_y_terms(ycols, weights, result):
    @pl.loop(0, KT)
    def _(k):
        cols = ycols.at[pl.ds(pl.multiple_of(k * ROWS, ROWS), (5 * KT + 1) * ROWS)]
        out = result.at[pl.ds(pl.multiple_of(k * CELLS, CELLS), CELLS)]
        for side in range(2):
            step = 2 * side - 1
            for half in range(2):
                span = pl.ds(8 * half * SIDE + side * (SIDE - 1), 8, stride=SIDE)
                total = out[span, :]
                for oz in OFFSETS:
                    for ox in OFFSETS:
                        at = (side * 3 + oz + 1) * KT * ROWS + Y0 + 8 * half + ox
                        total += cols[at : at + 8, :] * weights[tap_index(ox, step, oz)]
                out[span, :] = total


def add_corner_terms(values, hx, hy, tapsb, result):
    span = pl.ds(hx * (SIDE - 1) * SIDE + hy * (SIDE - 1), KT, stride=CELLS)
    total = result[span, :]
    for oz, value in enumerate(values):
        tap = tap_index(2 * hx - 1, 2 * hy - 1, oz - 1)
        total += value * tapsb[8 * tap : 8 * tap + 8, :]
    result[span, :] = total


def tap_products(field, grads, taps):
    def body(k, totals):
        totals = dict(zip(taps, totals))
        rows = field.at[pl.ds(pl.multiple_of(k * ROWS, ROWS), 3 * FIELD - (KT - 1) * ROWS)]
        own = grads.at[pl.ds(pl.multiple_of(k * CELLS, CELLS), CELLS)]
        for half in range(2):
            for slot in range(SIDE + 2):
                near = {}
                for ox in OFFSETS:
                    x = slot - 1 - ox
                    if 0 <= x < SIDE:
                        start = x * SIDE + 8 * half
                        near[ox] = own[start : start + 8, :]
                for oz in OFFSETS:
                    for oy in OFFSETS:
                        wanted = [ox for ox in near if (ox, oy, oz) in totals]
                        if not wanted:
                            continue
                        start = (oz + 1) * FIELD + slot * SLOT + Y0 + 8 * half + oy
                        value = rows[start : start + 8, :]
                        for ox in wanted:
                            totals[(ox, oy, oz)] = totals[(ox, oy, oz)] + value * near[ox]
        return tuple(totals[tap] for tap in taps)

    zero = jnp.zeros((8, 128), F32)
    return list(lax.fori_loop(0, KT, body, (zero,) * len(taps)))


TAPS = [(ox, oy, oz) for oz in OFFSETS for oy in OFFSETS for ox in OFFSETS]
GROUPS = (TAPS[:16], TAPS[16:])


def kernel(
    n_gx, n_gy,
    feat_hbm, map_ref, taps_hbm, gain_hbm, mix_hbm, cot_hbm,
    mixed, gf, tap_sums, mix_sums,
    taps_ref, gain_ref, mix_ref, feat, cot,
    field, gfield, depth, grads, ycols, normb, gnorm, scale, xsend2, tapsb, wdiag, mixacc, gainacc,
    xrecv1, yrecv1, crecv1, xrecv2, yrecv2, crecv2, ysend, csend, ysend2, csend2,
    msend, mrecv1, mpart, mrecv2, tsend, trecv1, tpart, trecv2,
    io_sem, send1, land1, send2, land2, rsend, rland,
):
    gx = lax.axis_index("gx")
    gy = lax.axis_index("gy")

    load_feat = pltpu.make_async_copy(feat_hbm, feat, io_sem.at[0])
    load_cot = pltpu.make_async_copy(cot_hbm, cot, io_sem.at[1])
    load_params = [
        pltpu.make_async_copy(src, dst, io_sem.at[2 + n])
        for n, (src, dst) in enumerate(
            ((taps_hbm, taps_ref), (gain_hbm, gain_ref), (mix_hbm, mix_ref))
        )
    ]

    def peer_x(d):
        return lax.rem(gx + d + n_gx, n_gx)

    def peer_y(d):
        return lax.rem(gy + d + n_gy, n_gy)

    barrier = pltpu.get_barrier_semaphore()

    def greet(dx, dy):
        pl.semaphore_signal(
            barrier, inc=1, device_id=(peer_x(dx), peer_y(dy)), device_id_type=MESH
        )

    around = [(dx, dy) for dx in OFFSETS for dy in OFFSETS if (dx, dy) != (0, 0)]
    for dx, dy in around:
        greet(dx, dy)
    load_feat.start()
    for copy in load_params:
        copy.start()
    load_cot.start()

    @pl.loop(2, n_gx - 1)
    def _(d):
        greet(d, 0)

    @pl.loop(2, n_gy - 1)
    def _(d):
        greet(0, d)

    low = lax.broadcasted_iota(jnp.int32, (SIDE, 128), 1) < CH
    low8 = low[:8]

    def level(i, j):
        return jnp.where(map_ref[i, 1, j] == 0, 1, 0)

    own_level = level(gx, gy)
    masks = {}
    for dx, dy in around:
        inside = (gx + dx >= 0) & (gx + dx < n_gx) & (gy + dy >= 0) & (gy + dy < n_gy)
        delta = level(peer_x(dx), peer_y(dy)) - own_level
        masks[(dx, dy)] = tuple(
            jnp.where(inside & (delta == step), 1.0, 0.0).astype(F32) for step in (0, -1, 1)
        )

    load_feat.wait()
    fill_own(lambda x, k: feat[x, :, k * 128 : (k + 1) * 128].astype(F32), field, low)
    gather_edges(
        lambda k, y: field[pl.ds(zrow(1, 1, k) + Y0 + y, SIDE, stride=SLOT), :],
        lambda x, y: field[pl.ds(zrow(1, 1 + x, 0) + Y0 + y, KT, stride=ROWS), :],
        ysend, csend,
    )

    def halo_copies(src, ys, cs, xr, yr, cr, send, land):
        copies = []
        for far in range(2):
            step = 2 * far - 1
            copies.append((src(far), xr.at[1 - far], (peer_x(step), gy)))
            copies.append((ys.at[far], yr.at[1 - far], (gx, peer_y(step))))
        for dx in (-1, 1):
            for dy in (-1, 1):
                here = (dx + 1) + (dy + 1) // 2
                copies.append((cs.at[here], cr.at[3 - here], (peer_x(dx), peer_y(dy))))
        return [
            pltpu.make_async_remote_copy(
                src_ref=a, dst_ref=b, send_sem=send.at[n], recv_sem=land.at[n],
                device_id=to, device_id_type=MESH,
            )
            for n, (a, b, to) in enumerate(copies)
        ]

    pl.semaphore_wait(barrier, (n_gx - 1) + (n_gy - 1) + 4)
    halo1 = halo_copies(
        lambda far: feat.at[far * (SIDE - 1)], ysend, csend, xrecv1, yrecv1, crecv1, send1, land1
    )
    for copy in halo1:
        copy.start()

    for copy in load_params:
        copy.wait()
    taps2 = jnp.concatenate([taps_ref[...], taps_ref[...]], axis=1)
    for tap in range(27):
        tapsb[8 * tap : 8 * tap + 8, :] = jnp.broadcast_to(taps2[tap : tap + 1, :], (8, 128))
    gain2 = jnp.concatenate([gain_ref[...], gain_ref[...]], axis=1)
    gain4 = jnp.concatenate([gain2, gain2], axis=1)
    row_block = lax.broadcasted_iota(jnp.int32, (4 * CH, 4 * CH), 0) // CH
    col_block = lax.broadcasted_iota(jnp.int32, (4 * CH, 4 * CH), 1) // CH
    diagonal = row_block == col_block
    wide = jnp.concatenate([mix_ref[...].astype(F32)] * 2, axis=1)
    wide = jnp.concatenate([wide, wide], axis=1)
    wide = jnp.concatenate([wide] * 4, axis=0)
    wdiag[0] = jnp.where(diagonal, wide, 0.0).astype(BF16)
    wdiag[1] = jnp.where(diagonal, 1.0 / CH, 0.0).astype(BF16)
    mixacc[...] = jnp.zeros_like(mixacc)
    gainacc[...] = jnp.zeros_like(gainacc)
    zero_halo(field, ycols)
    weights = [tapsb[8 * tap : 8 * tap + 8, :] for tap in range(27)]
    stencil(field, weights, depth, 0, KT)
    load_cot.wait()

    def wide_lanes(m):
        return pl.ds(pl.multiple_of(m * 256, 256), 256)

    @pl.loop(0, KT // 2)
    def _(m):
        gnorm[m] = lax.dot_general(
            cot[:, :, wide_lanes(m)].reshape(CELLS, 256), wdiag[0],
            (((1,), (1,)), ((), ())), preferred_element_type=F32,
        )

    for far in range(2):
        halo1[2 * far].wait_recv()
        fill_x(field, xrecv1, 1 - far, masks[(1 - 2 * far, 0)], low)
    add_x_terms(field, weights, depth)
    for far in range(2):
        halo1[2 * far + 1].wait_recv()
        fill_y(field, yrecv1, 1 - far, masks[(0, 1 - 2 * far)], low, ycols)
    add_y_terms(ycols, weights, depth)
    for copy in halo1[4:]:
        copy.wait_recv()
    for hx in range(2):
        for hy in range(2):
            values = fill_corner(field, crecv1, hx, hy, masks[(2 * hx - 1, 2 * hy - 1)], low)
            add_corner_terms(values, hx, hy, tapsb, depth)

    def tiles_of(m):
        return [pl.ds(pl.multiple_of((2 * m + h) * CELLS, CELLS), CELLS) for h in range(2)]

    @pl.loop(0, KT // 2, step=2)
    def _(first):
        for m in (first, first + 1):
            lanes = wide_lanes(m)
            values = jnp.concatenate([depth[tile, :] for tile in tiles_of(m)], axis=1)
            mean_square = jnp.dot(
                (values * values).astype(BF16), wdiag[1], preferred_element_type=F32
            )
            inv_rms = lax.rsqrt(mean_square + EPS)
            normed = values * inv_rms
            norm_bf = (normed * gain4).astype(BF16)
            scale[m] = inv_rms
            normb[:, lanes] = norm_bf
            mixacc[...] += lax.dot_general(
                norm_bf, cot[:, :, lanes].reshape(CELLS, 256),
                (((0,), (0,)), ((), ())), preferred_element_type=F32,
            )

    even = mixacc[0:CH, 0:128] + mixacc[2 * CH : 3 * CH, 128:256]
    odd = mixacc[CH : 2 * CH, 0:128] + mixacc[3 * CH : 4 * CH, 128:256]
    wide_low = lax.broadcasted_iota(jnp.int32, (CH, 128), 1) < CH
    both = jnp.where(wide_low, even, odd)
    both = both + pltpu.roll(both, CH, 1)
    packed = jnp.where(wide_low[:32], both[:32], both[32:])
    msend[...] = packed.astype(BF16)
    mrecv1[gy] = msend[...]

    def remote(src, dst, index, to):
        return pltpu.make_async_remote_copy(
            src_ref=src, dst_ref=dst, send_sem=rsend.at[index], recv_sem=rland.at[index],
            device_id=to, device_id_type=MESH,
        )

    def landed(buffer, index):
        pltpu.make_async_copy(buffer, buffer, rland.at[index]).wait()

    @pl.loop(1, n_gy)
    def _(d):
        remote(msend, mrecv1.at[gy], 0, (gx, peer_y(d))).start()

    @pl.loop(0, KT // 2, step=2)
    def _(first):
        for m in (first, first + 1):
            lanes = wide_lanes(m)
            inv_rms = scale[m]
            values = jnp.concatenate([depth[tile, :] for tile in tiles_of(m)], axis=1)
            normed = values * inv_rms
            grad_norm = gnorm[m]
            product = grad_norm * normed
            gainacc[...] += jnp.sum(product.reshape(CELLS // 8, 8, 256), axis=0)
            mean = jnp.dot((product * gain4).astype(BF16), wdiag[1], preferred_element_type=F32)
            grad_depth = (inv_rms * (grad_norm * gain4 - normed * mean)).astype(BF16)
            for far in range(2):
                start = far * SIDE * (SIDE - 1)
                xsend2[far, :, lanes] = grad_depth[start : start + SIDE]
            for h, tile in enumerate(tiles_of(m)):
                grads[tile, :] = grad_depth[:, h * 128 : (h + 1) * 128].astype(F32)

    for group, taps in enumerate(GROUPS):
        totals = tap_products(field, grads, taps)
        if group == 1:
            totals.append(gainacc[:, :128] + gainacc[:, 128:])
        rows = []
        for j in range(len(totals) // 2):
            pair = jnp.where(
                low8,
                totals[2 * j] + pltpu.roll(totals[2 * j], CH, 1),
                totals[2 * j + 1] + pltpu.roll(totals[2 * j + 1], CH, 1),
            )
            rows.append(jnp.sum(pair, axis=0, keepdims=True))
        rows += [jnp.zeros((1, 128), F32)] * (8 - len(rows))
        tsend[group] = jnp.concatenate(rows, axis=0).astype(BF16)
        trecv1[group, gx] = tsend[group]

        @pl.loop(1, n_gx)
        def _(d):
            remote(tsend.at[group], trecv1.at[group, gx], 2 + group, (peer_x(d), gy)).start()

    gather_edges(
        lambda k, y: grads[pl.ds(k * CELLS + y, SIDE, stride=SIDE), :],
        lambda x, y: grads[pl.ds(x * SIDE + y, KT, stride=CELLS), :],
        ysend2, csend2,
    )
    halo2 = halo_copies(
        lambda far: xsend2.at[far], ysend2, csend2, xrecv2, yrecv2, crecv2, send2, land2
    )
    for copy in halo2:
        copy.start()

    fill_own(
        lambda x, k: grads[pl.ds(pl.multiple_of(k * CELLS + x * SIDE, SIDE), SIDE), :],
        gfield, low,
    )

    @pl.loop(0, KT // 2)
    def _(m):
        lanes = wide_lanes(m)
        branch = jnp.dot(normb[:, lanes], wdiag[0], preferred_element_type=F32)
        inputs = feat[:, :, lanes].reshape(CELLS, 256).astype(F32)
        mixed[:, :, lanes] = (inputs + branch).astype(BF16).reshape(SIDE, SIDE, 256)

    def finish(k, out):
        lanes = pl.ds(pl.multiple_of(k * 128, 128), 128)
        for x in range(SIDE):
            total = cot[x, :, lanes].astype(F32) + out[x * SIDE : (x + 1) * SIDE, :]
            gf[x, :, lanes] = total.astype(BF16)

    landed(mrecv1.at[pl.ds(0, n_gy - 1)], 0)
    mpart[...] = jnp.sum(mrecv1[...].astype(F32), axis=0).astype(BF16)
    mrecv2[gx] = mpart[...]

    @pl.loop(1, n_gx)
    def _(d):
        remote(mpart, mrecv2.at[gx], 1, (peer_x(d), gy)).start()

    for group in range(2):
        landed(trecv1.at[group, pl.ds(0, n_gx - 1)], 2 + group)
        tpart[group] = jnp.sum(trecv1[group].astype(F32), axis=0).astype(BF16)
        trecv2[group, gy] = tpart[group]

        @pl.loop(1, n_gy)
        def _(d):
            remote(tpart.at[group], trecv2.at[group, gy], 4 + group, (gx, peer_y(d))).start()

    for copy in halo2:
        copy.wait_recv()
    for side in range(2):
        fill_x(gfield, xrecv2, side, masks[(2 * side - 1, 0)], low)
        fill_y(gfield, yrecv2, side, masks[(0, 2 * side - 1)], low)
        for hy in range(2):
            fill_corner(gfield, crecv2, side, hy, masks[(2 * side - 1, 2 * hy - 1)], low)

    stencil(gfield, weights[::-1], depth, 0, KT, finish)
    def sent(buffer, index):
        pltpu.make_async_copy(buffer, buffer, rsend.at[index]).wait()

    for copy in halo1 + halo2:
        copy.wait_send()
    sent(mrecv1.at[pl.ds(0, n_gy - 1)], 0)
    landed(mrecv2.at[pl.ds(0, n_gx - 1)], 1)
    mix_sums[...] = jnp.sum(mrecv2[...].astype(F32), axis=0)
    sent(mrecv2.at[pl.ds(0, n_gx - 1)], 1)
    for group in range(2):
        sent(trecv1.at[group, pl.ds(0, n_gx - 1)], 2 + group)
        landed(trecv2.at[group, pl.ds(0, n_gy - 1)], 4 + group)
        tap_sums[group] = jnp.sum(trecv2[group].astype(F32), axis=0)
        sent(trecv2.at[group, pl.ds(0, n_gy - 1)], 4 + group)

def deliver(
    mixed, gf, tap_sums, mix_sums, mixed_hbm, gf_hbm, gt_hbm, gg_hbm, gm_hbm,
    gt_ref, gg_ref, gm_ref, sem,
):
    copies = [
        pltpu.make_async_copy(src, dst, sem.at[n])
        for n, (src, dst) in enumerate(
            (
                (mixed, mixed_hbm), (gf, gf_hbm),
                (gt_ref, gt_hbm), (gg_ref, gg_hbm), (gm_ref, gm_hbm),
            )
        )
    ]
    copies[0].start()
    copies[1].start()
    for group, taps in enumerate(GROUPS):
        rows = tap_sums[group]
        turned = pltpu.roll(rows, CH, 1)
        for place, tap in enumerate(taps):
            source = turned if place % 2 else rows
            row = tap_index(*tap)
            gt_ref[row : row + 1, :] = source[place // 2 : place // 2 + 1, :CH]
        if group == 1:
            gg_ref[...] = turned[5:6, :CH]
    gm_ref[0:32, :] = mix_sums[:, :CH]
    gm_ref[32:64, :] = pltpu.roll(mix_sums[...], CH, 1)[:, :CH]
    for copy in copies[2:]:
        copy.start()
    for copy in copies:
        copy.wait()


def shards(n_gx, n_gy, features, slot_map, tap_weights, gain, mix_weight, cotangent):
    block = (SIDE, SIDE, LANES)
    vmem = pl.BlockSpec(memory_space=pltpu.VMEM)
    hbm = pl.BlockSpec(memory_space=pltpu.HBM)
    smem = pl.BlockSpec(memory_space=pltpu.SMEM)
    halo = [
        pltpu.VMEM((2, SIDE, LANES), BF16),
        pltpu.VMEM((2, SIDE, LANES), BF16),
        pltpu.VMEM((4, KT, 128), F32),
    ]
    sums = (jax.ShapeDtypeStruct((2, 8, 128), F32), jax.ShapeDtypeStruct((32, 128), F32))
    mixed, grad_features, tap_sums, mix_sums = pl.pallas_call(
        functools.partial(kernel, n_gx, n_gy),
        out_shape=(
            jax.ShapeDtypeStruct(block, BF16), jax.ShapeDtypeStruct(block, BF16), *sums
        ),
        in_specs=[hbm, smem, hbm, hbm, hbm, hbm],
        out_specs=(vmem,) * 4,
        scratch_shapes=[
            pltpu.VMEM((27, CH), F32), pltpu.VMEM((1, CH), F32), pltpu.VMEM((CH, CH), BF16),
            pltpu.VMEM(block, BF16),
            pltpu.VMEM(block, BF16),
            pltpu.VMEM((3 * FIELD, 128), F32),
            pltpu.VMEM((3 * FIELD, 128), F32),
            pltpu.VMEM((KT * CELLS, 128), F32),
            pltpu.VMEM((KT * CELLS, 128), F32),
            pltpu.VMEM((6 * KT * ROWS, 128), F32),
            pltpu.VMEM((CELLS, LANES), BF16),
            pltpu.VMEM((4, CELLS, 256), F32),
            pltpu.VMEM((4, CELLS, 256), F32),
            pltpu.VMEM((2, SIDE, LANES), BF16),
            pltpu.VMEM((27 * 8, 128), F32),
            pltpu.VMEM((2, 4 * CH, 4 * CH), BF16),
            pltpu.VMEM((4 * CH, 4 * CH), F32),
            pltpu.VMEM((8, 4 * CH), F32),
        ]
        + halo
        + halo
        + halo[1:]
        + halo[1:]
        + [
            pltpu.VMEM((32, 128), BF16),
            pltpu.VMEM((n_gy, 32, 128), BF16),
            pltpu.VMEM((32, 128), BF16),
            pltpu.VMEM((n_gx, 32, 128), BF16),
            pltpu.VMEM((2, 8, 128), BF16),
            pltpu.VMEM((2, n_gx, 8, 128), BF16),
            pltpu.VMEM((2, 8, 128), BF16),
            pltpu.VMEM((2, n_gy, 8, 128), BF16),
            pltpu.SemaphoreType.DMA((5,)),
            pltpu.SemaphoreType.DMA((8,)),
            pltpu.SemaphoreType.DMA((8,)),
            pltpu.SemaphoreType.DMA((8,)),
            pltpu.SemaphoreType.DMA((8,)),
            pltpu.SemaphoreType.DMA((6,)),
            pltpu.SemaphoreType.DMA((6,)),
        ],
        compiler_params=pltpu.CompilerParams(
            collective_id=0, has_side_effects=True, vmem_limit_bytes=40 * 1024 * 1024
        ),
        name="block_conv",
    )(
        *(
            pltpu.with_memory_space_constraint(value, pltpu.HBM)
            for value in (
                features.reshape(block), slot_map.transpose(0, 2, 1), tap_weights,
                gain.reshape(1, CH), mix_weight, cotangent.reshape(block),
            )
        )
    )
    mixed, grad_features, grad_taps, grad_gain, grad_mix = pl.pallas_call(
        deliver,
        out_shape=(
            jax.ShapeDtypeStruct(block, BF16),
            jax.ShapeDtypeStruct(block, BF16),
            jax.ShapeDtypeStruct((27, CH), F32),
            jax.ShapeDtypeStruct((1, CH), F32),
            jax.ShapeDtypeStruct((CH, CH), F32),
        ),
        in_specs=[vmem] * 4,
        out_specs=(hbm,) * 5,
        scratch_shapes=[
            pltpu.VMEM((27, CH), F32), pltpu.VMEM((1, CH), F32), pltpu.VMEM((CH, CH), F32),
            pltpu.SemaphoreType.DMA((5,)),
        ],
        compiler_params=pltpu.CompilerParams(vmem_limit_bytes=4 * 1024 * 1024),
        name="deliver",
    )(mixed, grad_features, tap_sums, mix_sums)
    return (
        mixed.reshape(features.shape), grad_features.reshape(features.shape),
        grad_taps, grad_gain.reshape(CH), grad_mix,
    )


def solution(mesh):
    return jax.shard_map(
        functools.partial(shards, mesh.shape["gx"], mesh.shape["gy"]),
        mesh=mesh,
        in_specs=(P("gx", "gy", None, None), P(), P(), P(), P(), P("gx", "gy", None, None)),
        out_specs=(P("gx", "gy", None, None), P("gx", "gy", None, None), P(), P(), P()),
        check_vma=False,
    )
```

```python
import functools

import jax
import jax.numpy as jnp
from jax import lax
from jax.experimental import pallas as pl
from jax.experimental.pallas import tpu as pltpu
from jax.sharding import PartitionSpec as P

EPS = 1e-05
MESH = pl.DeviceIdType.MESH
F32 = jnp.float32
BF16 = jnp.bfloat16
SIDE = 16
CH = 64
KT = 8
LANES = KT * 128
ROWS = 32
SLOT = KT * ROWS
FIELD = (SIDE + 2) * SLOT
Y0 = 8
CELLS = SIDE * SIDE
OFFSETS = (-1, 0, 1)


def zrow(oz, slot, tile):
    return oz * FIELD + slot * SLOT + tile * ROWS


def shifted_tiles(tiles, low):
    count = len(tiles)
    rot = [pltpu.roll(tile, CH, 1) for tile in tiles]
    down = [jnp.where(low, rot[k - 1], rot[k]) for k in range(count)]
    up = [jnp.where(low, rot[k], rot[(k + 1) % count]) for k in range(count)]
    return down, up


def fill_own(tile_of, field, low):
    @pl.loop(0, SIDE, step=2)
    def _(first):
        for x in (first, first + 1):
            tiles = [tile_of(x, k) for k in range(KT)]
            down, up = shifted_tiles(tiles, low)
            down[0] = jnp.where(low, 0.0, down[0])
            up[-1] = jnp.where(low, up[-1], 0.0)
            for oz, values in enumerate((down, tiles, up)):
                rows = field.at[pl.ds(pl.multiple_of(oz * FIELD + (x + 1) * SLOT, SLOT), SLOT)]
                for k in range(KT):
                    rows[k * ROWS + Y0 : k * ROWS + Y0 + SIDE, :] = values[k]


def zero_halo(field, ycols):
    zero = jnp.zeros((8, 128), F32)
    for oz in range(3):
        for slot in (0, SIDE + 1):
            field[zrow(oz, slot, 0) : zrow(oz, slot, 0) + SLOT, :] = jnp.zeros((SLOT, 128), F32)

    @pl.loop(0, SIDE)
    def _(x):
        for oz in range(3):
            rows = field.at[pl.ds(pl.multiple_of(oz * FIELD + (x + 1) * SLOT, SLOT), SLOT)]
            for k in range(KT):
                rows[k * ROWS : k * ROWS + 8, :] = zero
                rows[k * ROWS + 24 : k * ROWS + 32, :] = zero

    @pl.loop(0, 6 * KT)
    def _(group):
        rows = ycols.at[pl.ds(pl.multiple_of(group * ROWS, ROWS), ROWS)]
        rows[0:8, :] = zero
        rows[24:32, :] = zero


def gather_edges(column, corner, ysend, csend):
    for side in range(2):
        for k in range(KT):
            values = column(k, side * (SIDE - 1))
            ysend[side, :, k * 128 : (k + 1) * 128] = values.astype(BF16)
    for hx in range(2):
        for hy in range(2):
            csend[2 * hx + hy] = corner(hx * (SIDE - 1), hy * (SIDE - 1))


def masked_shifts(tiles, mask, low):
    same, below, above = mask
    down, up = shifted_tiles(tiles, low)
    first = jnp.where(low, below, same)
    last = jnp.where(low, same, above)
    down = [v * (first if k == 0 else same) for k, v in enumerate(down)]
    up = [v * (last if k == KT - 1 else same) for k, v in enumerate(up)]
    return down, [v * same for v in tiles], up


def fill_x(field, xrecv, side, mask, low):
    tiles = [xrecv[side, :, k * 128 : (k + 1) * 128].astype(F32) for k in range(KT)]
    for oz, values in enumerate(masked_shifts(tiles, mask, low)):
        for k in range(KT):
            start = zrow(oz, side * (SIDE + 1), k) + Y0
            field[start : start + SIDE, :] = values[k]


def fill_y(field, yrecv, side, mask, low, ycols=None):
    tiles = [yrecv[side, :, k * 128 : (k + 1) * 128].astype(F32) for k in range(KT)]
    for oz, values in enumerate(masked_shifts(tiles, mask, low)):
        for k in range(KT):
            start = zrow(oz, 1, k) + (Y0 - 1, Y0 + SIDE)[side]
            field[pl.ds(start, SIDE, stride=SLOT), :] = values[k]
            if ycols is not None:
                start = ((side * 3 + oz) * KT + k) * ROWS + Y0
                ycols[start : start + SIDE, :] = values[k]


def fill_corner(field, crecv, hx, hy, mask, low):
    low8 = low[:KT]
    row8 = lax.broadcasted_iota(jnp.int32, (KT, 128), 0)
    same, below, above = mask
    cell = crecv[2 * hx + hy]
    rot = pltpu.roll(cell, CH, 1)
    down = jnp.where(low8, pltpu.roll(rot, 1, 0), rot)
    up = jnp.where(low8, rot, pltpu.roll(rot, KT - 1, 0))
    down = down * jnp.where(low8 & (row8 == 0), below, same)
    up = up * jnp.where((~low8) & (row8 == KT - 1), above, same)
    values = (down, cell * same, up)
    for oz, value in enumerate(values):
        start = zrow(oz, hx * (SIDE + 1), 0) + (Y0 - 1, Y0 + SIDE)[hy]
        field[pl.ds(start, KT, stride=ROWS), :] = value
    return values


def tap_index(ox, oy, oz):
    return 9 * (ox + 1) + 3 * (oy + 1) + oz + 1


def stencil(field, weights, result, first, last, finish=None):
    @pl.loop(first, last)
    def _(k):
        rows = field.at[pl.ds(pl.multiple_of(k * ROWS, ROWS), 3 * FIELD - (KT - 1) * ROWS)]
        out = result.at[pl.ds(pl.multiple_of(k * CELLS, CELLS), CELLS)]
        for half in range(2):
            sums = {}
            for slot in range(SIDE + 2):
                for oz in OFFSETS:
                    for oy in OFFSETS:
                        start = (oz + 1) * FIELD + slot * SLOT + Y0 + 8 * half + oy
                        value = rows[start : start + 8, :]
                        for ox in OFFSETS:
                            x = slot - 1 - ox
                            if 0 <= x < SIDE:
                                term = value * weights[tap_index(ox, oy, oz)]
                                sums[x] = sums[x] + term if x in sums else term
                if slot >= 2:
                    start = (slot - 2) * SIDE + 8 * half
                    out[start : start + 8, :] = sums.pop(slot - 2)
        if finish is not None:
            finish(k, out)


def add_x_terms(field, weights, result):
    @pl.loop(0, KT)
    def _(k):
        rows = field.at[pl.ds(pl.multiple_of(k * ROWS, ROWS), 3 * FIELD - (KT - 1) * ROWS)]
        out = result.at[pl.ds(pl.multiple_of(k * CELLS, CELLS), CELLS)]
        for side in range(2):
            step = 2 * side - 1
            for half in range(2):
                start = side * (SIDE - 1) * SIDE + 8 * half
                total = out[start : start + 8, :]
                for oz in OFFSETS:
                    for oy in OFFSETS:
                        at = (oz + 1) * FIELD + side * (SIDE + 1) * SLOT + Y0 + 8 * half + oy
                        total += rows[at : at + 8, :] * weights[tap_index(step, oy, oz)]
                out[start : start + 8, :] = total


def add_y_terms(ycols, weights, result):
    @pl.loop(0, KT)
    def _(k):
        cols = ycols.at[pl.ds(pl.multiple_of(k * ROWS, ROWS), (5 * KT + 1) * ROWS)]
        out = result.at[pl.ds(pl.multiple_of(k * CELLS, CELLS), CELLS)]
        for side in range(2):
            step = 2 * side - 1
            for half in range(2):
                span = pl.ds(8 * half * SIDE + side * (SIDE - 1), 8, stride=SIDE)
                total = out[span, :]
                for oz in OFFSETS:
                    for ox in OFFSETS:
                        at = (side * 3 + oz + 1) * KT * ROWS + Y0 + 8 * half + ox
                        total += cols[at : at + 8, :] * weights[tap_index(ox, step, oz)]
                out[span, :] = total


def add_corner_terms(values, hx, hy, tapsb, result):
    span = pl.ds(hx * (SIDE - 1) * SIDE + hy * (SIDE - 1), KT, stride=CELLS)
    total = result[span, :]
    for oz, value in enumerate(values):
        tap = tap_index(2 * hx - 1, 2 * hy - 1, oz - 1)
        total += value * tapsb[8 * tap : 8 * tap + 8, :]
    result[span, :] = total


def tap_products(field, grads, taps):
    def body(k, totals):
        totals = dict(zip(taps, totals))
        rows = field.at[pl.ds(pl.multiple_of(k * ROWS, ROWS), 3 * FIELD - (KT - 1) * ROWS)]
        own = grads.at[pl.ds(pl.multiple_of(k * CELLS, CELLS), CELLS)]
        for half in range(2):
            for slot in range(SIDE + 2):
                near = {}
                for ox in OFFSETS:
                    x = slot - 1 - ox
                    if 0 <= x < SIDE:
                        start = x * SIDE + 8 * half
                        near[ox] = own[start : start + 8, :]
                for oz in OFFSETS:
                    for oy in OFFSETS:
                        wanted = [ox for ox in near if (ox, oy, oz) in totals]
                        if not wanted:
                            continue
                        start = (oz + 1) * FIELD + slot * SLOT + Y0 + 8 * half + oy
                        value = rows[start : start + 8, :]
                        for ox in wanted:
                            totals[(ox, oy, oz)] = totals[(ox, oy, oz)] + value * near[ox]
        return tuple(totals[tap] for tap in taps)

    zero = jnp.zeros((8, 128), F32)
    return list(lax.fori_loop(0, KT, body, (zero,) * len(taps)))


TAPS = [(ox, oy, oz) for oz in OFFSETS for oy in OFFSETS for ox in OFFSETS]
GROUPS = (TAPS[:16], TAPS[16:])


def kernel(
    n_gx, n_gy,
    feat_hbm, map_ref, taps_hbm, gain_hbm, mix_hbm, cot_hbm,
    mixed, gf, tap_sums, mix_sums,
    taps_ref, gain_ref, mix_ref, feat, cot,
    field, gfield, depth, grads, ycols, normb, gnorm, scale, xsend2, tapsb, wdiag, mixacc, gainacc,
    xrecv1, yrecv1, crecv1, xrecv2, yrecv2, crecv2, ysend, csend, ysend2, csend2,
    msend, mrecv1, mpart, mrecv2, tsend, trecv1, tpart, trecv2,
    io_sem, send1, land1, send2, land2, rsend, rland,
):
    gx = lax.axis_index("gx")
    gy = lax.axis_index("gy")

    load_feat = pltpu.make_async_copy(feat_hbm, feat, io_sem.at[0])
    load_cot = pltpu.make_async_copy(cot_hbm, cot, io_sem.at[1])
    load_params = [
        pltpu.make_async_copy(src, dst, io_sem.at[2 + n])
        for n, (src, dst) in enumerate(
            ((taps_hbm, taps_ref), (gain_hbm, gain_ref), (mix_hbm, mix_ref))
        )
    ]

    def peer_x(d):
        return lax.rem(gx + d + n_gx, n_gx)

    def peer_y(d):
        return lax.rem(gy + d + n_gy, n_gy)

    barrier = pltpu.get_barrier_semaphore()

    def greet(dx, dy):
        pl.semaphore_signal(
            barrier, inc=1, device_id=(peer_x(dx), peer_y(dy)), device_id_type=MESH
        )

    around = [(dx, dy) for dx in OFFSETS for dy in OFFSETS if (dx, dy) != (0, 0)]
    for dx, dy in around:
        greet(dx, dy)
    load_feat.start()
    for copy in load_params:
        copy.start()
    load_cot.start()

    @pl.loop(2, n_gx - 1)
    def _(d):
        greet(d, 0)

    @pl.loop(2, n_gy - 1)
    def _(d):
        greet(0, d)

    low = lax.broadcasted_iota(jnp.int32, (SIDE, 128), 1) < CH
    low8 = low[:8]

    def level(i, j):
        return jnp.where(map_ref[i, 1, j] == 0, 1, 0)

    own_level = level(gx, gy)
    masks = {}
    for dx, dy in around:
        inside = (gx + dx >= 0) & (gx + dx < n_gx) & (gy + dy >= 0) & (gy + dy < n_gy)
        delta = level(peer_x(dx), peer_y(dy)) - own_level
        masks[(dx, dy)] = tuple(
            jnp.where(inside & (delta == step), 1.0, 0.0).astype(F32) for step in (0, -1, 1)
        )

    load_feat.wait()
    fill_own(lambda x, k: feat[x, :, k * 128 : (k + 1) * 128].astype(F32), field, low)
    gather_edges(
        lambda k, y: field[pl.ds(zrow(1, 1, k) + Y0 + y, SIDE, stride=SLOT), :],
        lambda x, y: field[pl.ds(zrow(1, 1 + x, 0) + Y0 + y, KT, stride=ROWS), :],
        ysend, csend,
    )

    def halo_copies(src, ys, cs, xr, yr, cr, send, land):
        copies = []
        for far in range(2):
            step = 2 * far - 1
            copies.append((src(far), xr.at[1 - far], (peer_x(step), gy)))
            copies.append((ys.at[far], yr.at[1 - far], (gx, peer_y(step))))
        for dx in (-1, 1):
            for dy in (-1, 1):
                here = (dx + 1) + (dy + 1) // 2
                copies.append((cs.at[here], cr.at[3 - here], (peer_x(dx), peer_y(dy))))
        return [
            pltpu.make_async_remote_copy(
                src_ref=a, dst_ref=b, send_sem=send.at[n], recv_sem=land.at[n],
                device_id=to, device_id_type=MESH,
            )
            for n, (a, b, to) in enumerate(copies)
        ]

    pl.semaphore_wait(barrier, (n_gx - 1) + (n_gy - 1) + 4)
    halo1 = halo_copies(
        lambda far: feat.at[far * (SIDE - 1)], ysend, csend, xrecv1, yrecv1, crecv1, send1, land1
    )
    for copy in halo1:
        copy.start()

    for copy in load_params:
        copy.wait()
    taps2 = jnp.concatenate([taps_ref[...], taps_ref[...]], axis=1)
    for tap in range(27):
        tapsb[8 * tap : 8 * tap + 8, :] = jnp.broadcast_to(taps2[tap : tap + 1, :], (8, 128))
    gain2 = jnp.concatenate([gain_ref[...], gain_ref[...]], axis=1)
    gain4 = jnp.concatenate([gain2, gain2], axis=1)
    row_block = lax.broadcasted_iota(jnp.int32, (4 * CH, 4 * CH), 0) // CH
    col_block = lax.broadcasted_iota(jnp.int32, (4 * CH, 4 * CH), 1) // CH
    diagonal = row_block == col_block
    wide = jnp.concatenate([mix_ref[...].astype(F32)] * 2, axis=1)
    wide = jnp.concatenate([wide, wide], axis=1)
    wide = jnp.concatenate([wide] * 4, axis=0)
    wdiag[0] = jnp.where(diagonal, wide, 0.0).astype(BF16)
    wdiag[1] = jnp.where(diagonal, 1.0 / CH, 0.0).astype(BF16)
    mixacc[...] = jnp.zeros_like(mixacc)
    gainacc[...] = jnp.zeros_like(gainacc)
    zero_halo(field, ycols)
    weights = [tapsb[8 * tap : 8 * tap + 8, :] for tap in range(27)]
    stencil(field, weights, depth, 0, KT)
    load_cot.wait()

    def wide_lanes(m):
        return slice(256 * m, 256 * m + 256) if isinstance(m, int) else pl.ds(pl.multiple_of(m * 256, 256), 256)

    @pl.loop(0, KT // 2)
    def _(m):
        gnorm[m] = lax.dot_general(
            cot[:, :, wide_lanes(m)].reshape(CELLS, 256), wdiag[0],
            (((1,), (1,)), ((), ())), preferred_element_type=F32,
        )

    for far in range(2):
        halo1[2 * far].wait_recv()
        fill_x(field, xrecv1, 1 - far, masks[(1 - 2 * far, 0)], low)
    add_x_terms(field, weights, depth)
    for far in range(2):
        halo1[2 * far + 1].wait_recv()
        fill_y(field, yrecv1, 1 - far, masks[(0, 1 - 2 * far)], low, ycols)
    add_y_terms(ycols, weights, depth)
    for copy in halo1[4:]:
        copy.wait_recv()
    for hx in range(2):
        for hy in range(2):
            values = fill_corner(field, crecv1, hx, hy, masks[(2 * hx - 1, 2 * hy - 1)], low)
            add_corner_terms(values, hx, hy, tapsb, depth)

    def tiles_of(m):
        if isinstance(m, int):
            return [slice((2 * m + h) * CELLS, (2 * m + h + 1) * CELLS) for h in range(2)]
        return [pl.ds(pl.multiple_of((2 * m + h) * CELLS, CELLS), CELLS) for h in range(2)]

    @pl.loop(0, KT // 2, step=4)
    def _(first):
        for m in range(4):
            lanes = wide_lanes(m)
            values = jnp.concatenate([depth[tile, :] for tile in tiles_of(m)], axis=1)
            mean_square = jnp.dot(
                (values * values).astype(BF16), wdiag[1], preferred_element_type=F32
            )
            inv_rms = lax.rsqrt(mean_square + EPS)
            normed = values * inv_rms
            norm_bf = (normed * gain4).astype(BF16)
            scale[m] = inv_rms
            normb[:, lanes] = norm_bf
            mixacc[...] += lax.dot_general(
                norm_bf, cot[:, :, lanes].reshape(CELLS, 256),
                (((0,), (0,)), ((), ())), preferred_element_type=F32,
            )

    even = mixacc[0:CH, 0:128] + mixacc[2 * CH : 3 * CH, 128:256]
    odd = mixacc[CH : 2 * CH, 0:128] + mixacc[3 * CH : 4 * CH, 128:256]
    wide_low = lax.broadcasted_iota(jnp.int32, (CH, 128), 1) < CH
    both = jnp.where(wide_low, even, odd)
    both = both + pltpu.roll(both, CH, 1)
    packed = jnp.where(wide_low[:32], both[:32], both[32:])
    msend[...] = packed.astype(BF16)
    mrecv1[gy] = msend[...]

    def remote(src, dst, index, to):
        return pltpu.make_async_remote_copy(
            src_ref=src, dst_ref=dst, send_sem=rsend.at[index], recv_sem=rland.at[index],
            device_id=to, device_id_type=MESH,
        )

    def landed(buffer, index):
        pltpu.make_async_copy(buffer, buffer, rland.at[index]).wait()

    @pl.loop(1, n_gy)
    def _(d):
        remote(msend, mrecv1.at[gy], 0, (gx, peer_y(d))).start()

    @pl.loop(0, KT // 2, step=4)
    def _(first):
        for m in range(4):
            lanes = wide_lanes(m)
            inv_rms = scale[m]
            values = jnp.concatenate([depth[tile, :] for tile in tiles_of(m)], axis=1)
            normed = values * inv_rms
            grad_norm = gnorm[m]
            product = grad_norm * normed
            gainacc[...] += jnp.sum(product.reshape(CELLS // 8, 8, 256), axis=0)
            mean = jnp.dot((product * gain4).astype(BF16), wdiag[1], preferred_element_type=F32)
            grad_depth = (inv_rms * (grad_norm * gain4 - normed * mean)).astype(BF16)
            for far in range(2):
                start = far * SIDE * (SIDE - 1)
                xsend2[far, :, lanes] = grad_depth[start : start + SIDE]
            for h, tile in enumerate(tiles_of(m)):
                grads[tile, :] = grad_depth[:, h * 128 : (h + 1) * 128].astype(F32)

    for group, taps in enumerate(GROUPS):
        totals = tap_products(field, grads, taps)
        if group == 1:
            totals.append(gainacc[:, :128] + gainacc[:, 128:])
        rows = []
        for j in range(len(totals) // 2):
            pair = jnp.where(
                low8,
                totals[2 * j] + pltpu.roll(totals[2 * j], CH, 1),
                totals[2 * j + 1] + pltpu.roll(totals[2 * j + 1], CH, 1),
            )
            rows.append(jnp.sum(pair, axis=0, keepdims=True))
        rows += [jnp.zeros((1, 128), F32)] * (8 - len(rows))
        tsend[group] = jnp.concatenate(rows, axis=0).astype(BF16)
        trecv1[group, gx] = tsend[group]

        @pl.loop(1, n_gx)
        def _(d):
            remote(tsend.at[group], trecv1.at[group, gx], 2 + group, (peer_x(d), gy)).start()

    gather_edges(
        lambda k, y: grads[pl.ds(k * CELLS + y, SIDE, stride=SIDE), :],
        lambda x, y: grads[pl.ds(x * SIDE + y, KT, stride=CELLS), :],
        ysend2, csend2,
    )
    halo2 = halo_copies(
        lambda far: xsend2.at[far], ysend2, csend2, xrecv2, yrecv2, crecv2, send2, land2
    )
    for copy in halo2:
        copy.start()

    fill_own(
        lambda x, k: grads[pl.ds(pl.multiple_of(k * CELLS + x * SIDE, SIDE), SIDE), :],
        gfield, low,
    )

    @pl.loop(0, KT // 2)
    def _(m):
        lanes = wide_lanes(m)
        branch = jnp.dot(normb[:, lanes], wdiag[0], preferred_element_type=F32)
        inputs = feat[:, :, lanes].reshape(CELLS, 256).astype(F32)
        mixed[:, :, lanes] = (inputs + branch).astype(BF16).reshape(SIDE, SIDE, 256)

    def finish(k, out):
        lanes = pl.ds(pl.multiple_of(k * 128, 128), 128)
        for x in range(SIDE):
            total = cot[x, :, lanes].astype(F32) + out[x * SIDE : (x + 1) * SIDE, :]
            gf[x, :, lanes] = total.astype(BF16)

    landed(mrecv1.at[pl.ds(0, n_gy - 1)], 0)
    mpart[...] = jnp.sum(mrecv1[...].astype(F32), axis=0).astype(BF16)
    mrecv2[gx] = mpart[...]

    @pl.loop(1, n_gx)
    def _(d):
        remote(mpart, mrecv2.at[gx], 1, (peer_x(d), gy)).start()

    for group in range(2):
        landed(trecv1.at[group, pl.ds(0, n_gx - 1)], 2 + group)
        tpart[group] = jnp.sum(trecv1[group].astype(F32), axis=0)
        trecv2[group, gy] = tpart[group]

        @pl.loop(1, n_gy)
        def _(d):
            remote(tpart.at[group], trecv2.at[group, gy], 4 + group, (gx, peer_y(d))).start()

    for copy in halo2:
        copy.wait_recv()
    for side in range(2):
        fill_x(gfield, xrecv2, side, masks[(2 * side - 1, 0)], low)
        fill_y(gfield, yrecv2, side, masks[(0, 2 * side - 1)], low)
        for hy in range(2):
            fill_corner(gfield, crecv2, side, hy, masks[(2 * side - 1, 2 * hy - 1)], low)

    stencil(gfield, weights[::-1], depth, 0, KT, finish)
    def sent(buffer, index):
        pltpu.make_async_copy(buffer, buffer, rsend.at[index]).wait()

    for copy in halo1 + halo2:
        copy.wait_send()
    sent(mrecv1.at[pl.ds(0, n_gy - 1)], 0)
    landed(mrecv2.at[pl.ds(0, n_gx - 1)], 1)
    mix_sums[...] = jnp.sum(mrecv2[...].astype(F32), axis=0)
    sent(mrecv2.at[pl.ds(0, n_gx - 1)], 1)
    for group in range(2):
        sent(trecv1.at[group, pl.ds(0, n_gx - 1)], 2 + group)
        landed(trecv2.at[group, pl.ds(0, n_gy - 1)], 4 + group)
        tap_sums[group] = jnp.sum(trecv2[group], axis=0)
        sent(trecv2.at[group, pl.ds(0, n_gy - 1)], 4 + group)

def deliver(
    mixed, gf, tap_sums, mix_sums, mixed_hbm, gf_hbm, gt_hbm, gg_hbm, gm_hbm,
    gt_ref, gg_ref, gm_ref, sem,
):
    copies = [
        pltpu.make_async_copy(src, dst, sem.at[n])
        for n, (src, dst) in enumerate(
            (
                (mixed, mixed_hbm), (gf, gf_hbm),
                (gt_ref, gt_hbm), (gg_ref, gg_hbm), (gm_ref, gm_hbm),
            )
        )
    ]
    copies[0].start()
    copies[1].start()
    for group, taps in enumerate(GROUPS):
        rows = tap_sums[group]
        turned = pltpu.roll(rows, CH, 1)
        for place, tap in enumerate(taps):
            source = turned if place % 2 else rows
            row = tap_index(*tap)
            gt_ref[row : row + 1, :] = source[place // 2 : place // 2 + 1, :CH]
        if group == 1:
            gg_ref[...] = turned[5:6, :CH]
    gm_ref[0:32, :] = mix_sums[:, :CH]
    gm_ref[32:64, :] = pltpu.roll(mix_sums[...], CH, 1)[:, :CH]
    for copy in copies[2:]:
        copy.start()
    for copy in copies:
        copy.wait()


def shards(n_gx, n_gy, features, slot_map, tap_weights, gain, mix_weight, cotangent):
    block = (SIDE, SIDE, LANES)
    vmem = pl.BlockSpec(memory_space=pltpu.VMEM)
    hbm = pl.BlockSpec(memory_space=pltpu.HBM)
    smem = pl.BlockSpec(memory_space=pltpu.SMEM)
    halo = [
        pltpu.VMEM((2, SIDE, LANES), BF16),
        pltpu.VMEM((2, SIDE, LANES), BF16),
        pltpu.VMEM((4, KT, 128), F32),
    ]
    sums = (jax.ShapeDtypeStruct((2, 8, 128), F32), jax.ShapeDtypeStruct((32, 128), F32))
    mixed, grad_features, tap_sums, mix_sums = pl.pallas_call(
        functools.partial(kernel, n_gx, n_gy),
        out_shape=(
            jax.ShapeDtypeStruct(block, BF16), jax.ShapeDtypeStruct(block, BF16), *sums
        ),
        in_specs=[hbm, smem, hbm, hbm, hbm, hbm],
        out_specs=(vmem,) * 4,
        scratch_shapes=[
            pltpu.VMEM((27, CH), F32), pltpu.VMEM((1, CH), F32), pltpu.VMEM((CH, CH), BF16),
            pltpu.VMEM(block, BF16),
            pltpu.VMEM(block, BF16),
            pltpu.VMEM((3 * FIELD, 128), F32),
            pltpu.VMEM((3 * FIELD, 128), F32),
            pltpu.VMEM((KT * CELLS, 128), F32),
            pltpu.VMEM((KT * CELLS, 128), F32),
            pltpu.VMEM((6 * KT * ROWS, 128), F32),
            pltpu.VMEM((CELLS, LANES), BF16),
            pltpu.VMEM((4, CELLS, 256), F32),
            pltpu.VMEM((4, CELLS, 256), F32),
            pltpu.VMEM((2, SIDE, LANES), BF16),
            pltpu.VMEM((27 * 8, 128), F32),
            pltpu.VMEM((2, 4 * CH, 4 * CH), BF16),
            pltpu.VMEM((4 * CH, 4 * CH), F32),
            pltpu.VMEM((8, 4 * CH), F32),
        ]
        + halo
        + halo
        + halo[1:]
        + halo[1:]
        + [
            pltpu.VMEM((32, 128), BF16),
            pltpu.VMEM((n_gy, 32, 128), BF16),
            pltpu.VMEM((32, 128), BF16),
            pltpu.VMEM((n_gx, 32, 128), BF16),
            pltpu.VMEM((2, 8, 128), BF16),
            pltpu.VMEM((2, n_gx, 8, 128), BF16),
            pltpu.VMEM((2, 8, 128), F32),
            pltpu.VMEM((2, n_gy, 8, 128), F32),
            pltpu.SemaphoreType.DMA((5,)),
            pltpu.SemaphoreType.DMA((8,)),
            pltpu.SemaphoreType.DMA((8,)),
            pltpu.SemaphoreType.DMA((8,)),
            pltpu.SemaphoreType.DMA((8,)),
            pltpu.SemaphoreType.DMA((6,)),
            pltpu.SemaphoreType.DMA((6,)),
        ],
        compiler_params=pltpu.CompilerParams(
            collective_id=0, has_side_effects=True, vmem_limit_bytes=40 * 1024 * 1024
        ),
        name="block_conv",
    )(
        *(
            pltpu.with_memory_space_constraint(value, pltpu.HBM)
            for value in (
                features.reshape(block), slot_map.transpose(0, 2, 1), tap_weights,
                gain.reshape(1, CH), mix_weight, cotangent.reshape(block),
            )
        )
    )
    mixed, grad_features, grad_taps, grad_gain, grad_mix = pl.pallas_call(
        deliver,
        out_shape=(
            jax.ShapeDtypeStruct(block, BF16),
            jax.ShapeDtypeStruct(block, BF16),
            jax.ShapeDtypeStruct((27, CH), F32),
            jax.ShapeDtypeStruct((1, CH), F32),
            jax.ShapeDtypeStruct((CH, CH), F32),
        ),
        in_specs=[vmem] * 4,
        out_specs=(hbm,) * 5,
        scratch_shapes=[
            pltpu.VMEM((27, CH), F32), pltpu.VMEM((1, CH), F32), pltpu.VMEM((CH, CH), F32),
            pltpu.SemaphoreType.DMA((5,)),
        ],
        compiler_params=pltpu.CompilerParams(vmem_limit_bytes=4 * 1024 * 1024),
        name="deliver",
    )(mixed, grad_features, tap_sums, mix_sums)
    return (
        mixed.reshape(features.shape), grad_features.reshape(features.shape),
        grad_taps, grad_gain.reshape(CH), grad_mix,
    )


def solution(mesh):
    return jax.shard_map(
        functools.partial(shards, mesh.shape["gx"], mesh.shape["gy"]),
        mesh=mesh,
        in_specs=(P("gx", "gy", None, None), P(), P(), P(), P(), P("gx", "gy", None, None)),
        out_specs=(P("gx", "gy", None, None), P("gx", "gy", None, None), P(), P(), P()),
        check_vma=False,
    )
```
